512 devices in a mesh: row: 16 (over z), col: 32 (over x, y, core).
Axes of the slice: x: 4, y: 4, z: 16, core: 2. Of those that a mesh axis runs over, the one named last changes fastest.
Arguments:
- hidden_in: bfloat16 [4096, 1792], P('col', 'row'), may hold values from -6 to 6
- attn_gain: float32 [1792], replicated, may hold values from 0.1 to 1.9
- mlp_gain: float32 [1792], replicated, may hold values from 0.1 to 1.9
- w_query: bfloat16 [1792, 256], P(None, 'row'), may hold values from -0.125 to 0.125
- w_key: bfloat16 [1792, 256], P(None, 'row'), may hold values from -0.125 to 0.125
- w_value: bfloat16 [1792, 1792], P(None, 'row'), may hold values from -0.125 to 0.125
- w_out: bfloat16 [1792, 1792], P('row'), may hold values from -0.1875 to 0.1875
- w_gate: bfloat16 [1792, 3584], P(None, 'row'), may hold values from -0.125 to 0.125
- w_up: bfloat16 [1792, 3584], P(None, 'row'), may hold values from -0.125 to 0.125
- w_down: bfloat16 [3584, 1792], P('row'), may hold values from -0.125 to 0.125
- page_states: bfloat16 [512, 16, 273, 112], P('col', 'row'), may hold values from -16 to 16
- page_norms: float32 [512, 16, 273], P('col', 'row'), as said below
- page_home: int32 [512, 1], P('col'), may hold values from 0 to 31; in each aligned block of 16 rows (0 to 15, 16 to 31, ...) at most 2 rows name the same one
- page_request: int32 [512], P('col'), may hold values from 0 to 1
- parents: int32 [64, 64], P('col'), may hold values from 0 to 62, as said below
- accepted: int32 [64], P('col'), may hold values from 0 to 63
Outputs:
- hidden_out: bfloat16 [4096, 1792], P('col', 'row')
- new_states: bfloat16 [64, 16, 273, 112], P('col', 'row')
- new_norms: float32 [64, 16, 273], P('col', 'row')
The draws below stay inside these ranges and needn't reach their ends.
Inputs may be any that keep to these rules, and one draw needn't show every extreme that they name: Among the 16 slots of one device at most 2 have the same page_home, and in every draw some device has exactly 2. parents[r, 0] = 0, parents[r, i] < i for i >= 1, and the last node's parent is the node before it. Each page_norms[s, h] is a factor of 2 to 16 times the mean of phi over eight vectors, so phi(u) . page_norms[s, h] >= 1 for every vector u.
All inputs are finite; a program needn't handle non-finite values.
Results may differ from the reference program's by a relative error of at most 0.023.
Values may be sent and summed in bfloat16 or wider, within the bound.
No kernel may reach another device: no remote copies, remote signals or barrier semaphores. Data moves between devices by JAX's collectives and lax.ppermute only.
A program may use at most 64 MiB of HBM per device.

```python
import math
import jax
import jax.numpy as jnp
import numpy as np
from jax import lax

D = 1792
H = 16
FD = 16
DV = 112
F = 273
FF = 3584
NODES = 64
REQ_DEV = 2
SLOTS_DEV = 16
CAP = 2
REQS = 64
SLOTS = 512
TOKENS = 4096
N_ROW = 16
N_COL = 32


def feature_map_drawn(vectors):
    width_in = vectors.shape[-1]
    linear = vectors * width_in ** (-0.25)
    square = vectors[..., :, None] * vectors[..., None, :] * (2.0 * width_in) ** (-0.5)
    square = square.reshape(vectors.shape[:-1] + (width_in * width_in,))
    leading = jnp.ones(vectors.shape[:-1] + (1,), vectors.dtype)
    return jnp.concatenate([leading, linear, square], axis=-1)


def draw_page_norms(key, part):
    key_vectors, key_factor = jax.random.split(jax.random.fold_in(key, 11))
    samples = jax.random.normal(key_vectors, (SLOTS, H, 8, FD), jnp.float32)
    factor = jax.random.uniform(key_factor, (SLOTS, H, 1), jnp.float32, 2.0, 16.0)
    return jnp.mean(feature_map_drawn(samples), axis=2) * factor


def draw_parents(key, part):
    node_ids = jnp.arange(NODES, dtype=jnp.int32)
    upper_bound = jnp.maximum(node_ids, 1)
    picked = jax.random.randint(jax.random.fold_in(key, 23), (REQS, NODES), 0, upper_bound[None, :])
    picked = jnp.where(node_ids[None, :] == NODES - 1, NODES - 2, picked)
    return jnp.where(node_ids[None, :] == 0, 0, picked).astype(jnp.int32)


def with_ends(result, rng, low, top_value):
    index_at = [jax.random.randint(jax.random.fold_in(rng, axis), (), 0, length) for axis, length in enumerate(result.shape)]
    main_axis = result.shape.index(max(result.shape))
    next_to = index_at[:main_axis] + [(index_at[main_axis] + 1) % result.shape[main_axis]] + index_at[main_axis + 1:]
    return result.at[tuple(index_at)].set(low).at[tuple(next_to)].set(top_value)


def spiked(entries, own_key, source, target, blocks, factor):
    owner, partner = [(jnp.arange(entries.shape[dim]) // (entries.shape[dim] // blocks)).reshape([-1 if axis == dim else 1 for axis in range(entries.ndim)]) for dim in (source, target)]
    chosen = jax.random.permutation(own_key, blocks)[partner]
    strong = (owner == chosen) | (owner == (partner + blocks // 2) % blocks)
    return jnp.where(strong, factor * entries, entries)


def steps_of(key, shape, shards, low, largest):
    loudness = 1.0
    for dim, parts in shards:
        steps = jax.random.uniform(jax.random.fold_in(jax.random.fold_in(key, 6), dim), (parts,), jnp.float32, low / len(shards), largest / len(shards))
        loudness = loudness * jnp.repeat(jnp.exp(steps), shape[dim] // parts).reshape((-1,) + (1,) * (len(shape) - 1 - dim))
    return loudness


def deal_out(stream_key, own, number, rows, number_of, top, limit, slope):
    ranking = jax.random.permutation(stream_key, number_of)
    crowded, usual = shares(number_of, rows * top, limit, slope, True), shares(number_of, rows * top, limit, slope, False)
    places = jnp.arange(number_of)

    def named(lengths, turn):
        used = int((lengths > 0).sum())
        fixed = max(1, used // 4)
        moved = fixed + (places - fixed + turn * (used - fixed)) % max(1, number_of - fixed)
        return jnp.zeros((number_of,), jnp.int32).at[ranking[jnp.where(places < fixed, places, moved)]].set(jnp.asarray(lengths, jnp.int32))

    lengths = jnp.where(number % 4 == 0, named(crowded, number // 4), named(usual, number - number // 4 - 1))
    mixed = jax.random.permutation(jax.random.fold_in(own, 3), number_of)
    donor, receiver = mixed[0:number_of // 2 * 2:2], mixed[1:number_of // 2 * 2:2]
    room = jnp.minimum(lengths[donor] - 1, limit - lengths[receiver]) // 2
    room = jnp.where((donor == ranking[0]) | (receiver == ranking[0]) | (lengths[receiver] == 0), 0, jnp.maximum(room, 0))
    moved = jax.random.randint(jax.random.fold_in(own, 4), (number_of // 2,), 0, 1 << 20) % (room + 1)
    lengths = lengths.at[donor].add(-moved).at[receiver].add(moved)
    members = jnp.searchsorted(jnp.cumsum(lengths), jnp.arange(rows * top), side="right").astype(jnp.int32)
    table = members.reshape(top, rows).T
    table = table[jax.random.permutation(jax.random.fold_in(own, 1), rows)]
    turn = jax.random.randint(jax.random.fold_in(own, 2), (rows, 1), 0, top)
    return jnp.take_along_axis(table, (jnp.arange(top)[None, :] + turn) % top, axis=1)


def shares(count, total, limit, slope, full):
    portions = [(1 << 20) // math.isqrt(grade ** slope) + 1 for grade in range(1, count + 1)]
    largest = limit if full else min(limit, max(-(-total // count), total * portions[0] // sum(portions)))
    least = 1 if total - largest >= count - 1 else 0
    counts, rest = [largest] + [least] * (count - 1), total - largest - least * (count - 1)
    while rest > 0:
        free = [i for i in range(1, count) if counts[i] < largest] or [i for i in range(1, count) if counts[i] < limit]
        pool, left = sum([portions[i] for i in free]), rest
        for i in free:
            more = min(limit - counts[i], max(1, left * portions[i] // pool), rest)
            counts[i] = counts[i] + more
            rest = rest - more
    return np.array(counts)


def scatter_about(key, dims, deviation, limit, cuts=(), kind=jnp.bfloat16):
    drawn = jax.random.normal(key, dims, jnp.float32) * deviation
    if len(cuts) > 0:
        drawn = steps_of(key, dims, cuts, -0.22, 0.18) * drawn
    return jnp.clip(drawn, min=-limit, max=limit).astype(kind)


def bell_draw_with(rng, dims, spread, limit, pieces, heavy, kind=jnp.bfloat16):
    array = spread * jax.random.normal(rng, dims, jnp.float32)
    if pieces:
        array = array * steps_of(rng, dims, pieces, -0.22, 0.18)
    return jnp.clip(spiked(array, jax.random.fold_in(rng, 3), *heavy), -limit, limit).astype(kind)


def setup_inputs(seed: int = 0) -> dict:
    splits = jax.random.split(jax.random.key(seed), 17)
    hidden_in = scatter_about(splits[0], (TOKENS, D), 1.0, 6.0, ((0, 32), (1, 16)))
    attn_gain = jnp.clip(1.0 + 0.18 * jax.random.normal(splits[1], (D,), jnp.float32), 0.1, 1.9)
    mlp_gain = jnp.clip(1.0 + 0.18 * jax.random.normal(splits[2], (D,), jnp.float32), 0.1, 1.9)
    w_query = scatter_about(splits[3], (D, H * FD), D ** -0.5, 0.125, ((1, 16),))
    w_key = scatter_about(splits[4], (D, H * FD), D ** -0.5, 0.125, ((1, 16),))
    w_value = scatter_about(splits[5], (D, H * DV), D ** -0.5, 0.125, ((1, 16),))
    w_out = bell_draw_with(splits[6], (H * DV, D), (H * DV) ** -0.5, 0.1875, ((0, 16),), (0, 1, 16, 2.0))
    w_gate = scatter_about(splits[7], (D, FF), D ** -0.5, 0.125, ((1, 16),))
    w_up = scatter_about(splits[8], (D, FF), D ** -0.5, 0.125, ((1, 16),))
    w_down = bell_draw_with(splits[9], (FF, D), FF ** -0.5, 0.125, ((0, 16),), (0, 1, 16, 2.0))
    page_states = scatter_about(splits[10], (SLOTS, H, F, DV), 4.0, 16.0, ((0, 32), (1, 16)))
    page_norms = draw_page_norms(jax.random.fold_in(splits[16], 71), 0)
    page_home_keys = jax.random.split(jax.random.fold_in(splits[12], 1), SLOTS // SLOTS_DEV)
    page_home_turns = jax.random.permutation(jax.random.fold_in(splits[12], 3), SLOTS // SLOTS_DEV)
    page_home = jax.vmap(lambda own, number: deal_out(jax.random.fold_in(splits[12], 2), own, number, SLOTS_DEV, N_COL, 1, CAP, 2))(page_home_keys, page_home_turns).reshape((SLOTS, 1))
    page_request = with_ends(jax.random.randint(splits[13], (SLOTS,), 0, REQ_DEV), jax.random.fold_in(splits[13], 1), 0, REQ_DEV - 1).astype(jnp.int32)
    parents = draw_parents(jax.random.fold_in(splits[16], 71), 0)
    accepted = with_ends(jax.random.randint(splits[15], (REQS,), 0, NODES), jax.random.fold_in(splits[15], 1), 0, NODES - 1).astype(jnp.int32)
    return dict(hidden_in=hidden_in, attn_gain=attn_gain, mlp_gain=mlp_gain, w_query=w_query, w_key=w_key, w_value=w_value, w_out=w_out, w_gate=w_gate, w_up=w_up, w_down=w_down, page_states=page_states, page_norms=page_norms, page_home=page_home, page_request=page_request, parents=parents, accepted=accepted)


epsilon = 1e-05

def feature_map(vectors):
    width_in = vectors.shape[-1]
    linear = vectors * width_in ** (-0.25)
    square = vectors[..., :, None] * vectors[..., None, :] * (2.0 * width_in) ** (-0.5)
    square = square.reshape(vectors.shape[:-1] + (width_in * width_in,))
    leading = jnp.ones(vectors.shape[:-1] + (1,), vectors.dtype)
    return jnp.concatenate([leading, linear, square], axis=-1)

def rms_norm(hidden, gain):
    mean_square = lax.optimization_barrier(jnp.mean(hidden * hidden, axis=-1, keepdims=True))
    return hidden * lax.rsqrt(mean_square + epsilon) * gain

def ancestors(parents):
    nodes = parents.shape[-1]
    node_ids = jnp.arange(nodes, dtype=jnp.int32)
    linked = (parents[..., :, None] == node_ids[None, :]) | (node_ids[:, None] == node_ids[None, :])
    reached = linked.astype(jnp.float32)
    for repeat in range(max(1, (nodes - 1).bit_length())):
        reached = jnp.minimum(jnp.einsum('rij,rjk->rik', reached, reached, precision=lax.Precision.HIGHEST), 1.0)
    return reached

def project_groups(inputs, weight, groups):
    block_width = inputs.shape[1] // groups
    summed = jnp.zeros((inputs.shape[0], weight.shape[1]), jnp.float32)
    for group_index in range(groups):
        lower = group_index * block_width
        partial_value = jnp.dot(inputs[:, lower:lower + block_width], weight[lower:lower + block_width], preferred_element_type=jnp.float32)
        summed = summed + lax.optimization_barrier(partial_value.astype(jnp.bfloat16)).astype(jnp.float32)
    return summed

def reference(hidden_in, attn_gain, mlp_gain, w_query, w_key, w_value, w_out, w_gate, w_up, w_down, page_states, page_norms, page_home, page_request, parents, accepted):
    highest = lax.Precision.HIGHEST
    hidden = hidden_in.astype(jnp.float32)
    normed = rms_norm(hidden, attn_gain).astype(jnp.bfloat16)
    queries = jnp.dot(normed, w_query, preferred_element_type=jnp.float32).astype(jnp.bfloat16)
    key_rows = jnp.dot(normed, w_key, preferred_element_type=jnp.float32).astype(jnp.bfloat16)
    values = jnp.dot(normed, w_value, preferred_element_type=jnp.float32).astype(jnp.bfloat16)
    query_heads = queries.astype(jnp.float32).reshape(REQS, NODES, H, FD)
    key_heads = key_rows.astype(jnp.float32).reshape(REQS, NODES, H, FD)
    value_heads = values.astype(jnp.float32).reshape(REQS, NODES, H, DV)
    reached = ancestors(parents)
    scaled = jnp.einsum('rihf,rjhf->rhij', query_heads, key_heads, precision=highest) / math.sqrt(FD)
    kernel = (1.0 + scaled + 0.5 * scaled * scaled) * reached[:, None, :, :]
    tree_den = jnp.transpose(lax.optimization_barrier(jnp.sum(kernel, axis=-1)), (0, 2, 1))
    kernel_low = lax.optimization_barrier(kernel.astype(jnp.bfloat16)).astype(jnp.float32)
    tree_num = jnp.einsum('rhij,rjhd->rihd', kernel_low, value_heads, precision=highest)
    phi_query = feature_map(query_heads)
    phi_low = lax.optimization_barrier(phi_query.astype(jnp.bfloat16)).astype(jnp.float32)
    owners = (page_home[:, 0] * REQ_DEV + page_request).astype(jnp.int32)

    def add_page(carry, slot_data):
        num_total, den_total = carry
        state, norm_row, owner = slot_data
        rows_low = lax.dynamic_index_in_dim(phi_low, owner, 0, keepdims=False)
        rows_full = lax.dynamic_index_in_dim(phi_query, owner, 0, keepdims=False)
        numer = jnp.einsum('nhf,hfd->nhd', rows_low, state.astype(jnp.float32), precision=highest)
        denom = jnp.einsum('nhf,hf->nh', rows_full, norm_row, precision=highest)
        return ((num_total.at[owner].add(numer), den_total.at[owner].add(denom)), None)
    zero_num = jnp.zeros((REQS, NODES, H, DV), jnp.float32)
    zero_den = jnp.zeros((REQS, NODES, H), jnp.float32)
    (pref_num, pref_den), unused = lax.scan(add_page, (zero_num, zero_den), (page_states, page_norms, owners))
    mixed = ((pref_num + tree_num) / (pref_den + tree_den)[..., None]).astype(jnp.bfloat16)
    mixed = mixed.reshape(TOKENS, H * DV)
    attn = project_groups(mixed, w_out, N_ROW)
    residual = hidden + attn
    normed_mlp = rms_norm(residual, mlp_gain).astype(jnp.bfloat16)
    gate_proj = jnp.dot(normed_mlp, w_gate, preferred_element_type=jnp.float32)
    up_proj = jnp.dot(normed_mlp, w_up, preferred_element_type=jnp.float32)
    activated = (jax.nn.silu(gate_proj) * up_proj).astype(jnp.bfloat16)
    mlp_out = project_groups(activated, w_down, N_ROW)
    hidden_out = (residual + mlp_out).astype(jnp.bfloat16)
    node_ids = jnp.arange(NODES, dtype=jnp.int32)
    chosen = (node_ids[None, :] == accepted[:, None]).astype(jnp.float32)
    path_mask = jnp.einsum('ri,rij->rj', chosen, reached, precision=highest)
    phi_key = feature_map(key_heads)
    new_norms = jnp.einsum('rj,rjhf->rhf', path_mask, phi_key, precision=highest)
    phi_key_low = lax.optimization_barrier(phi_key.astype(jnp.bfloat16)).astype(jnp.float32)
    weighted = phi_key_low * path_mask[:, :, None, None]
    new_states = jnp.einsum('rjhf,rjhd->rhfd', weighted, value_heads, precision=highest).astype(jnp.bfloat16)
    return (hidden_out, new_states, new_norms)
```

```python
import numpy as np

import jax
import jax.numpy as jnp
from jax import lax
from jax.experimental import pallas as pl
from jax.experimental.pallas import tpu as pltpu
from jax.sharding import PartitionSpec as P

EPS = 1e-05
FD = 16
F = 1 + FD + FD * FD
PAIRS = [(a, b) for a in range(FD) for b in range(a, FD)]
NFOLD = 1 + FD + len(PAIRS)
RFOLD = 160
LIN = float(FD) ** (-0.25)
QUAD = (2.0 * FD) ** (-0.5)
BF = jnp.bfloat16
F32 = jnp.float32
HI = lax.Precision.HIGHEST
VMEM = pl.BlockSpec(memory_space=pltpu.VMEM)
SMEM = pl.BlockSpec(memory_space=pltpu.SMEM)
PARAMS = pltpu.CompilerParams(vmem_limit_bytes=56 * 1024 * 1024)


def fold_tables():
    first = np.zeros((RFOLD, FD), np.float32)
    second = np.zeros((RFOLD, FD), np.float32)
    fold = np.zeros((RFOLD, F), np.float32)
    fold[0, 0] = 1
    for a in range(FD):
        first[1 + a, a] = 1
        fold[1 + a, 1 + a] = 1
    for p, (a, b) in enumerate(PAIRS):
        row = 1 + FD + p
        first[row, a] = 1
        second[row, b] = 1
        fold[row, 1 + FD + FD * a + b] = 1
        fold[row, 1 + FD + FD * b + a] = 1
    return first, second, fold


def full_tables(copies, rows):
    first = np.zeros((rows, FD), np.float32)
    second = np.zeros((rows, FD), np.float32)
    for f in range(F):
        for c in range(copies):
            row = f * copies + c
            if 1 <= f <= FD:
                first[row, f - 1] = 1
            elif f > FD:
                first[row, (f - 1 - FD) // FD] = 1
                second[row, (f - 1 - FD) % FD] = 1
    return first, second


def dot(a, b, ca, cb, precision=None):
    return lax.dot_general(
        a, b, (((ca,), (cb,)), ((), ())), precision=precision, preferred_element_type=F32
    )


def iota(shape, dim):
    return lax.broadcasted_iota(jnp.int32, shape, dim)


def features(first, second, vec, shift, live):
    one = dot(first, vec, 1, 0)
    two = dot(second, vec, 1, 0)
    feat = iota(one.shape, 0) >> shift
    one = one + jnp.where(feat == 0, 1.0, 0.0)
    two = two + jnp.where(feat <= FD, 1.0, 0.0)
    scale = jnp.where(feat == 0, 1.0, jnp.where(feat <= FD, LIN, QUAD))
    return one * two * jnp.where(feat < live, scale, 0.0)


def pack_kernel(home, request, states, norms, fold, out, folded, slots):
    n_slots = states.shape[1]
    width = states.shape[2]
    lanes = out.shape[2]
    for f in range(1 + FD):
        folded[f] = states[f]
    for p, (a, b) in enumerate(PAIRS):
        one = states[1 + FD + FD * a + b]
        folded[1 + FD + p] = one if a == b else one + states[1 + FD + FD * b + a]
    folded[NFOLD:RFOLD] = jnp.zeros((RFOLD - NFOLD, n_slots, width), BF)
    block = 16
    side = block * n_slots
    row = iota((side, side), 0)
    turn = jnp.where(
        iota((side, side), 1) == (row % block) * n_slots + row // block, 1.0, 0.0
    ).astype(BF)
    for g in range(RFOLD // block):
        part = folded[g * block : (g + 1) * block].reshape(side, width)
        turned = dot(turn, part, 1, 0).astype(BF)
        slots[:, g * block : (g + 1) * block, 0:width] = turned.reshape(n_slots, block, width)
    spread = jnp.where(
        iota((n_slots, lanes), 1) == width + iota((n_slots, lanes), 0), 1.0, 0.0
    )
    by_lane = dot(spread, norms[...], 0, 0, HI)
    norm_lanes = dot(fold[...], by_lane, 1, 1, HI)
    out[...] = jnp.zeros(out.shape, out.dtype)
    lane = iota((RFOLD, lanes), 1)
    for s in range(n_slots):
        owner = home[s] * 2 + request[s]
        value = jnp.where(
            lane < width,
            slots[s].astype(F32),
            jnp.where(lane == width + s, norm_lanes, 0.0),
        )
        out[owner] = out[owner] + value.astype(BF)


def gain_columns(gain):
    n = gain.shape[0]
    padded = jnp.concatenate([gain[...], jnp.zeros((16 - n, 128), F32)], axis=0)
    return jnp.transpose(jnp.concatenate([padded] * 8, axis=0))


def normed_columns(load, n, gain):
    cols = gain_columns(gain)
    total = jnp.zeros((1, 128), F32)
    for j in range(n):
        block = load(j)
        total = total + jnp.sum(block * block, axis=0, keepdims=True)
    scale = lax.rsqrt(total / (n * 128) + EPS)
    return [
        (load(j) * scale * cols[:, j : j + 1]).astype(BF) for j in range(n)
    ]


def tree_kernel(hidden, gain, w_q, w_k, w_v, parents, accepted, first, second,
                phi_hi, phi_lo, tree_num, tree_den, keys, vals, path):
    n = gain.shape[0]
    normed = jnp.concatenate(
        normed_columns(
            lambda j: hidden[j * 128 : (j + 1) * 128].astype(F32), n, gain
        ),
        axis=0,
    )
    q = dot(w_q[...], normed, 1, 0).astype(BF)
    k = dot(w_k[...], normed, 1, 0).astype(BF)
    v = dot(w_v[...], normed, 1, 0).astype(BF)
    keys[...] = k
    vals[...] = v
    tok = q.shape[1]
    up = parents[...]
    row = iota((tok, tok), 0)
    col = iota((tok, tok), 1)
    reach = jnp.where((row == up) | (row == col), 1.0, 0.0)
    for repeat in range(6):
        low = reach.astype(BF)
        reach = jnp.minimum(dot(low, low, 1, 0), 1.0)
    scaled = dot(k, q, 0, 0) * (1.0 / FD**0.5)
    kernel = (1.0 + scaled + 0.5 * scaled * scaled) * reach
    tree_den[...] = jnp.broadcast_to(jnp.sum(kernel, axis=0, keepdims=True), tree_den.shape)
    tree_num[...] = dot(v, kernel.astype(BF), 1, 0)
    phi = features(first[...], second[...], q, 0, NFOLD)
    low = phi.astype(BF)
    phi_hi[...] = low
    phi_lo[...] = (phi - low.astype(F32)).astype(BF)
    lane8 = iota((8, tok), 1)
    sub8 = iota((8, tok), 0)
    half = tok // 2
    chosen = jnp.where(sub8 == 0, accepted[0], accepted[1] + half)
    pick = jnp.where((lane8 == chosen) & (sub8 < 2), 1.0, 0.0).astype(BF)
    path[...] = dot(pick, reach.astype(BF), 1, 1)


def page_kernel(keys, vals, path, first2, second2, first1, second1, states, norms):
    k = keys[...]
    phi = features(first2[...], second2[...], k, 1, F)
    mask = jnp.where(iota(phi.shape, 0) % 2 == 0, path[0:1], path[1:2])
    weighted = phi.astype(BF) * mask.astype(BF)
    states[...] = dot(weighted, vals[...], 1, 1).astype(BF)
    phi1 = features(first1[...], second1[...], k, 0, F)
    norms[...] = dot(path[...], phi1, 1, 1, HI)


def mix_kernel(got, phi_hi, phi_lo, tree_num, tree_den, out, total):
    step = pl.program_id(0)

    @pl.when(step == 0)
    def _():
        total[...] = jnp.zeros(total.shape, F32)

    for r in range(2):
        part = got[r].astype(F32)
        for i in range(1, got.shape[0] // 2):
            part = part + got[2 * i + r].astype(F32)
        total[r] = total[r] + part

    @pl.when(step == pl.num_programs(0) - 1)
    def _():
        width = tree_num.shape[0]
        high_phi = phi_hi[...]
        nums = []
        dens = []
        for r in range(2):
            whole = total[r]
            high = whole.astype(BF)
            low = (whole - high.astype(F32)).astype(BF)
            both = dot(high, high_phi, 0, 0) + dot(low, high_phi, 0, 0)
            extra = dot(high, phi_lo[...], 0, 0)
            nums.append(both[:width])
            dens.append(jnp.sum(both[width:] + extra[width:], axis=0, keepdims=True))
        lane = iota(nums[0].shape, 1)
        half = nums[0].shape[1] // 2
        num = jnp.where(lane < half, nums[0], nums[1])
        den = jnp.where(lane[0:1] < half, dens[0], dens[1])
        mixed = ((num + tree_num[...]) / (den + tree_den[0:1])).astype(BF)
        out[...] = jnp.broadcast_to(mixed[None], out.shape)


def mlp_kernel(row_ref, mixed, w_out, hidden, gain, w_gate, w_up, w_down,
               down, residual_own, residual):
    n = gain.shape[0]
    m = mixed[...]
    for j in range(n):
        rows = slice(j * 128, (j + 1) * 128)
        residual[rows] = hidden[rows].astype(F32) + dot(w_out[:, rows], m, 0, 0)
    own = residual_own.shape[0]
    residual_own[...] = residual[pl.ds(pl.multiple_of(row_ref[0] * own, 8), own)]
    normed = jnp.concatenate(
        normed_columns(lambda j: residual[j * 128 : (j + 1) * 128], n, gain), axis=0
    )
    gate = dot(w_gate[...], normed, 1, 0)
    up = dot(w_up[...], normed, 1, 0)
    active = (gate / (1.0 + jnp.exp(-gate)) * up).astype(BF)
    down[...] = dot(w_down[...], active, 0, 0).astype(BF)


def call(kernel, n_smem, args, outs, scratch=(), **extra):
    return pl.pallas_call(
        kernel,
        out_shape=outs,
        in_specs=[SMEM] * n_smem + [VMEM] * (len(args) - n_smem),
        out_specs=jax.tree.map(lambda _: VMEM, outs),
        scratch_shapes=scratch,
        compiler_params=PARAMS,
        **extra,
    )(*args)


def shape(dims, dtype):
    return jax.ShapeDtypeStruct(dims, dtype)


def local(
    hidden_in,
    attn_gain,
    mlp_gain,
    w_query,
    w_key,
    w_value,
    w_out,
    w_gate,
    w_up,
    w_down,
    page_states,
    page_norms,
    page_home,
    page_request,
    parents,
    accepted,
):
    n_row = lax.axis_size("row")
    n_col = lax.axis_size("col")
    tok, own = hidden_in.shape
    width = n_row * own
    value_width = w_value.shape[1]
    slot_count = page_states.shape[0]
    row = lax.axis_index("row").astype(jnp.int32).reshape(1)
    first, second, fold = fold_tables()
    first1, second1 = full_tables(1, 280)
    first2, second2 = full_tables(2, 560)
    first, second, first1, second1, first2, second2 = (
        jnp.asarray(t, BF) for t in (first, second, first1, second1, first2, second2)
    )

    all_out = lax.all_gather(w_out, "row", axis=0, tiled=True)

    packed = call(
        pack_kernel,
        2,
        (
            page_home.reshape(slot_count),
            page_request,
            jnp.transpose(page_states[:, 0], (1, 0, 2)),
            page_norms[:, 0],
            jnp.asarray(fold, F32),
        ),
        shape((2 * n_col, RFOLD, 128), BF),
        (
            pltpu.VMEM((RFOLD, slot_count, value_width), BF),
            pltpu.VMEM((slot_count, RFOLD, 128), BF),
        ),
    )
    packed, hidden_t = lax.optimization_barrier((packed, hidden_in.T))
    got = lax.all_to_all(packed, "col", split_axis=0, concat_axis=0, tiled=True)
    hidden = lax.all_gather(hidden_t, "row", axis=0, tiled=True)

    offsets = jnp.arange(parents.shape[0], dtype=jnp.int32)[:, None] * parents.shape[1]
    phi_hi, phi_lo, tree_num, tree_den, keys, vals, path = pl.pallas_call(
        tree_kernel,
        out_shape=(
            shape((RFOLD, tok), BF),
            shape((RFOLD, tok), BF),
            shape((value_width, tok), F32),
            shape((8, tok), F32),
            shape((FD, tok), BF),
            shape((value_width, tok), BF),
            shape((8, tok), F32),
        ),
        in_specs=[VMEM] * 6 + [SMEM] + [VMEM] * 2,
        out_specs=(VMEM,) * 7,
        compiler_params=PARAMS,
    )(
        hidden,
        attn_gain.reshape(-1, 128),
        w_query.T,
        w_key.T,
        w_value.T,
        (parents + offsets).reshape(1, tok),
        accepted,
        first,
        second,
    )

    steps = 4
    chunk = 2 * n_col // steps
    mixed_copies = pl.pallas_call(
        mix_kernel,
        grid=(steps,),
        out_shape=shape((n_row, value_width, tok), BF),
        in_specs=[
            pl.BlockSpec((chunk, RFOLD, 128), lambda i: (i, 0, 0)),
            pl.BlockSpec((RFOLD, tok), lambda i: (0, 0)),
            pl.BlockSpec((RFOLD, tok), lambda i: (0, 0)),
            pl.BlockSpec((value_width, tok), lambda i: (0, 0)),
            pl.BlockSpec((8, tok), lambda i: (0, 0)),
        ],
        out_specs=pl.BlockSpec((n_row, value_width, tok), lambda i: (0, 0, 0)),
        scratch_shapes=[pltpu.VMEM((2, RFOLD, 128), F32)],
        compiler_params=PARAMS,
    )(got, phi_hi, phi_lo, tree_num, tree_den)

    mixed = lax.all_to_all(mixed_copies, "row", split_axis=0, concat_axis=0, tiled=True)

    states, norms = call(
        page_kernel,
        0,
        (keys, vals, path, first2, second2, first1, second1),
        (shape((560, value_width), BF), shape((8, 280), F32)),
    )

    down, residual_own = call(
        mlp_kernel,
        1,
        (
            row,
            mixed.reshape(n_row * value_width, tok),
            all_out,
            hidden,
            mlp_gain.reshape(-1, 128),
            w_gate.T,
            w_up.T,
            w_down,
        ),
        (shape((width, tok), BF), shape((own, tok), F32)),
        (pltpu.VMEM((width, tok), F32),),
    )
    parts = lax.all_to_all(
        down.reshape(n_row, own, tok), "row", split_axis=0, concat_axis=0, tiled=True
    )
    hidden_out = (residual_own + jnp.sum(parts.astype(F32), axis=0)).astype(BF).T
    new_states = jnp.transpose(states[: 2 * F].reshape(F, 2, value_width), (1, 0, 2))[:, None]
    new_norms = norms[:2, :F][:, None]
    return (hidden_out, new_states, new_norms)


def solution(mesh):
    return jax.shard_map(
        local,
        mesh=mesh,
        in_specs=(
            P("col", "row"),
            P(),
            P(),
            P(None, "row"),
            P(None, "row"),
            P(None, "row"),
            P("row", None),
            P(None, "row"),
            P(None, "row"),
            P("row", None),
            P("col", "row", None, None),
            P("col", "row", None),
            P("col", None),
            P("col"),
            P("col", None),
            P("col"),
        ),
        out_specs=(P("col", "row"), P("col", "row", None, None), P("col", "row", None)),
        check_vma=False,
    )
```

```python
import numpy as np

import jax
import jax.numpy as jnp
from jax import lax
from jax.experimental import pallas as pl
from jax.experimental.pallas import tpu as pltpu
from jax.sharding import Mesh, PartitionSpec as P

EPS = 1e-05
COL = ("chip", "core")
FD = 16
F = 1 + FD + FD * FD
PAIRS = [(a, b) for a in range(FD) for b in range(a, FD)]
NFOLD = 1 + FD + len(PAIRS)
RFOLD = 160
LIN = float(FD) ** (-0.25)
QUAD = (2.0 * FD) ** (-0.5)
BF = jnp.bfloat16
F32 = jnp.float32
HI = lax.Precision.HIGHEST
VMEM = pl.BlockSpec(memory_space=pltpu.VMEM)
SMEM = pl.BlockSpec(memory_space=pltpu.SMEM)
PARAMS = pltpu.CompilerParams(vmem_limit_bytes=56 * 1024 * 1024)


def fold_tables():
    first = np.zeros((RFOLD, FD), np.float32)
    second = np.zeros((RFOLD, FD), np.float32)
    fold = np.zeros((RFOLD, F), np.float32)
    fold[0, 0] = 1
    for a in range(FD):
        first[1 + a, a] = 1
        fold[1 + a, 1 + a] = 1
    for p, (a, b) in enumerate(PAIRS):
        row = 1 + FD + p
        first[row, a] = 1
        second[row, b] = 1
        fold[row, 1 + FD + FD * a + b] = 1
        fold[row, 1 + FD + FD * b + a] = 1
    return first, second, fold


def full_tables(copies, rows):
    first = np.zeros((rows, FD), np.float32)
    second = np.zeros((rows, FD), np.float32)
    for f in range(F):
        for c in range(copies):
            row = f * copies + c
            if 1 <= f <= FD:
                first[row, f - 1] = 1
            elif f > FD:
                first[row, (f - 1 - FD) // FD] = 1
                second[row, (f - 1 - FD) % FD] = 1
    return first, second


def dot(a, b, ca, cb, precision=None):
    return lax.dot_general(
        a, b, (((ca,), (cb,)), ((), ())), precision=precision, preferred_element_type=F32
    )


def iota(shape, dim):
    return lax.broadcasted_iota(jnp.int32, shape, dim)


def features(first, second, vec, shift, live):
    one = dot(first, vec, 1, 0)
    two = dot(second, vec, 1, 0)
    feat = iota(one.shape, 0) >> shift
    one = one + jnp.where(feat == 0, 1.0, 0.0)
    two = two + jnp.where(feat <= FD, 1.0, 0.0)
    scale = jnp.where(feat == 0, 1.0, jnp.where(feat <= FD, LIN, QUAD))
    return one * two * jnp.where(feat < live, scale, 0.0)


def pack_kernel(home, request, states, norms, fold, out, folded, slots):
    n_slots = states.shape[1]
    width = states.shape[2]
    lanes = out.shape[2]
    for f in range(1 + FD):
        folded[f] = states[f]
    for p, (a, b) in enumerate(PAIRS):
        one = states[1 + FD + FD * a + b]
        folded[1 + FD + p] = one if a == b else one + states[1 + FD + FD * b + a]
    folded[NFOLD:RFOLD] = jnp.zeros((RFOLD - NFOLD, n_slots, width), BF)
    block = 16
    side = block * n_slots
    row = iota((side, side), 0)
    turn = jnp.where(
        iota((side, side), 1) == (row % block) * n_slots + row // block, 1.0, 0.0
    ).astype(BF)
    for g in range(RFOLD // block):
        part = folded[g * block : (g + 1) * block].reshape(side, width)
        turned = dot(turn, part, 1, 0).astype(BF)
        slots[:, g * block : (g + 1) * block, 0:width] = turned.reshape(n_slots, block, width)
    spread = jnp.where(
        iota((n_slots, lanes), 1) == width + iota((n_slots, lanes), 0), 1.0, 0.0
    )
    by_lane = dot(spread, norms[...], 0, 0, HI)
    norm_lanes = dot(fold[...], by_lane, 1, 1, HI)
    out[...] = jnp.zeros(out.shape, out.dtype)
    lane = iota((RFOLD, lanes), 1)
    for s in range(n_slots):
        owner = home[s] * 2 + request[s]
        value = jnp.where(
            lane < width,
            slots[s].astype(F32),
            jnp.where(lane == width + s, norm_lanes, 0.0),
        )
        out[owner] = out[owner] + value.astype(BF)


def gain_columns(gain):
    n = gain.shape[0]
    padded = jnp.concatenate([gain[...], jnp.zeros((16 - n, 128), F32)], axis=0)
    return jnp.transpose(jnp.concatenate([padded] * 8, axis=0))


def normed_columns(load, n, gain):
    cols = gain_columns(gain)
    total = jnp.zeros((1, 128), F32)
    for j in range(n):
        block = load(j)
        total = total + jnp.sum(block * block, axis=0, keepdims=True)
    scale = lax.rsqrt(total / (n * 128) + EPS)
    return [
        (load(j) * scale * cols[:, j : j + 1]).astype(BF) for j in range(n)
    ]


def tree_kernel(hidden, gain, w_q, w_k, w_v, parents, accepted, first, second,
                phi_hi, phi_lo, tree_num, tree_den, keys, vals, path):
    n = gain.shape[0]
    normed = jnp.concatenate(
        normed_columns(
            lambda j: hidden[j * 128 : (j + 1) * 128].astype(F32), n, gain
        ),
        axis=0,
    )
    q = dot(w_q[...], normed, 1, 0).astype(BF)
    k = dot(w_k[...], normed, 1, 0).astype(BF)
    v = dot(w_v[...], normed, 1, 0).astype(BF)
    keys[...] = k
    vals[...] = v
    tok = q.shape[1]
    up = parents[...]
    row = iota((tok, tok), 0)
    col = iota((tok, tok), 1)
    reach = jnp.where((row == up) | (row == col), 1.0, 0.0)
    for repeat in range(6):
        low = reach.astype(BF)
        reach = jnp.minimum(dot(low, low, 1, 0), 1.0)
    scaled = dot(k, q, 0, 0) * (1.0 / FD**0.5)
    kernel = (1.0 + scaled + 0.5 * scaled * scaled) * reach
    tree_den[...] = jnp.broadcast_to(jnp.sum(kernel, axis=0, keepdims=True), tree_den.shape)
    tree_num[...] = dot(v, kernel.astype(BF), 1, 0)
    phi = features(first[...], second[...], q, 0, NFOLD)
    low = phi.astype(BF)
    phi_hi[...] = low
    phi_lo[...] = (phi - low.astype(F32)).astype(BF)
    lane8 = iota((8, tok), 1)
    sub8 = iota((8, tok), 0)
    half = tok // 2
    chosen = jnp.where(sub8 == 0, accepted[0], accepted[1] + half)
    pick = jnp.where((lane8 == chosen) & (sub8 < 2), 1.0, 0.0).astype(BF)
    path[...] = dot(pick, reach.astype(BF), 1, 1)


def page_kernel(keys, vals, path, first2, second2, first1, second1, states, norms):
    k = keys[...]
    phi = features(first2[...], second2[...], k, 1, F)
    mask = jnp.where(iota(phi.shape, 0) % 2 == 0, path[0:1], path[1:2])
    weighted = phi.astype(BF) * mask.astype(BF)
    states[...] = dot(weighted, vals[...], 1, 1).astype(BF)
    phi1 = features(first1[...], second1[...], k, 0, F)
    norms[...] = dot(path[...], phi1, 1, 1, HI)


def mix_kernel(got, phi_hi, phi_lo, tree_num, tree_den, out):
    width = tree_num.shape[0]
    high_phi = phi_hi[...]
    low_phi = phi_lo[...]
    nums = []
    dens = []
    for r in range(2):
        whole = got[r].astype(F32)
        for i in range(1, got.shape[0] // 2):
            whole = whole + got[2 * i + r].astype(F32)
        high = whole.astype(BF)
        low = (whole - high.astype(F32)).astype(BF)
        both = dot(high, high_phi, 0, 0) + dot(low, high_phi, 0, 0)
        extra = dot(high, low_phi, 0, 0)
        nums.append(both[:width])
        dens.append(jnp.sum(both[width:] + extra[width:], axis=0, keepdims=True))
    lane = iota(nums[0].shape, 1)
    half = nums[0].shape[1] // 2
    num = jnp.where(lane < half, nums[0], nums[1])
    den = jnp.where(lane[0:1] < half, dens[0], dens[1])
    mixed = ((num + tree_num[...]) / (den + tree_den[0:1])).astype(BF)
    out[...] = mixed


def mlp_kernel(row_ref, mixed, w_out, hidden, gain, w_gate, w_up, w_down,
               down, residual_own, residual):
    n = gain.shape[0]
    m = mixed[...]
    for j in range(n):
        rows = slice(j * 128, (j + 1) * 128)
        residual[rows] = hidden[rows].astype(F32) + dot(w_out[:, rows], m, 0, 0)
    own = residual_own.shape[0]
    residual_own[...] = residual[pl.ds(pl.multiple_of(row_ref[0] * own, 8), own)]
    normed = jnp.concatenate(
        normed_columns(lambda j: residual[j * 128 : (j + 1) * 128], n, gain), axis=0
    )
    gate = dot(w_gate[...], normed, 1, 0)
    up = dot(w_up[...], normed, 1, 0)
    active = (gate / (1.0 + jnp.exp(-gate)) * up).astype(BF)
    down[...] = dot(w_down[...], active, 0, 0).astype(BF)


def call(kernel, n_smem, args, outs, scratch=(), **extra):
    return pl.pallas_call(
        kernel,
        out_shape=outs,
        in_specs=[SMEM] * n_smem + [VMEM] * (len(args) - n_smem),
        out_specs=jax.tree.map(lambda _: VMEM, outs),
        scratch_shapes=scratch,
        compiler_params=PARAMS,
        **extra,
    )(*args)


def in_vmem(x):
    return pltpu.with_memory_space_constraint(x, pltpu.VMEM)


def shape(dims, dtype):
    return jax.ShapeDtypeStruct(dims, dtype)


def local(
    hidden_in,
    attn_gain,
    mlp_gain,
    w_query,
    w_key,
    w_value,
    w_out,
    w_gate,
    w_up,
    w_down,
    page_states,
    page_norms,
    page_home,
    page_request,
    parents,
    accepted,
):
    n_row = lax.axis_size("row")
    n_col = lax.axis_size(COL)
    tok, own = hidden_in.shape
    width = n_row * own
    value_width = w_value.shape[1]
    slot_count = page_states.shape[0]
    row = lax.axis_index("row").astype(jnp.int32).reshape(1)
    first, second, fold = fold_tables()
    first1, second1 = full_tables(1, 280)
    first2, second2 = full_tables(2, 560)
    first, second, first1, second1, first2, second2 = (
        jnp.asarray(t, BF) for t in (first, second, first1, second1, first2, second2)
    )

    half = w_out.shape[0] // 2
    half_out = lax.dynamic_slice_in_dim(w_out, lax.axis_index("core") * half, half, 0)
    all_out = lax.all_gather(half_out, ("row", "core"), axis=0, tiled=True)

    packed = call(
        pack_kernel,
        2,
        (
            page_home.reshape(slot_count),
            page_request,
            jnp.transpose(page_states[:, 0], (1, 0, 2)),
            page_norms[:, 0],
            jnp.asarray(fold, F32),
        ),
        shape((2 * n_col, RFOLD, 128), BF),
        (
            pltpu.VMEM((RFOLD, slot_count, value_width), BF),
            pltpu.VMEM((slot_count, RFOLD, 128), BF),
        ),
    )
    packed, hidden_t = lax.optimization_barrier((packed, hidden_in.T))
    got = lax.all_to_all(packed, COL, split_axis=0, concat_axis=0, tiled=True)
    got = in_vmem(got)
    hidden = lax.all_gather(hidden_t, "row", axis=0, tiled=True)

    offsets = jnp.arange(parents.shape[0], dtype=jnp.int32)[:, None] * parents.shape[1]
    phi_hi, phi_lo, tree_num, tree_den, keys, vals, path = pl.pallas_call(
        tree_kernel,
        out_shape=(
            shape((RFOLD, tok), BF),
            shape((RFOLD, tok), BF),
            shape((value_width, tok), F32),
            shape((8, tok), F32),
            shape((FD, tok), BF),
            shape((value_width, tok), BF),
            shape((8, tok), F32),
        ),
        in_specs=[VMEM] * 6 + [SMEM] + [VMEM] * 2,
        out_specs=(VMEM,) * 7,
        compiler_params=PARAMS,
    )(
        hidden,
        attn_gain.reshape(-1, 128),
        w_query.T,
        w_key.T,
        w_value.T,
        (parents + offsets).reshape(1, tok),
        accepted,
        first,
        second,
    )

    mixed_own = call(
        mix_kernel,
        0,
        (got, phi_hi, phi_lo, tree_num, tree_den),
        shape((value_width, tok), BF),
    )

    mixed = lax.all_gather(mixed_own, "row", axis=0, tiled=True)

    states, norms = call(
        page_kernel,
        0,
        (keys, vals, path, first2, second2, first1, second1),
        (shape((560, value_width), BF), shape((8, 280), F32)),
    )

    down, residual_own = call(
        mlp_kernel,
        1,
        (
            row,
            in_vmem(mixed),
            all_out,
            hidden,
            mlp_gain.reshape(-1, 128),
            w_gate.T,
            w_up.T,
            w_down,
        ),
        (shape((width, tok), BF), shape((own, tok), F32)),
        (pltpu.VMEM((width, tok), F32),),
    )
    parts = lax.all_to_all(
        down.reshape(n_row, own, tok), "row", split_axis=0, concat_axis=0, tiled=True
    )
    hidden_out = (residual_own + jnp.sum(parts.astype(F32), axis=0)).astype(BF).T
    new_states = jnp.transpose(states[: 2 * F].reshape(F, 2, value_width), (1, 0, 2))[:, None]
    new_norms = norms[:2, :F][:, None]
    return (hidden_out, new_states, new_norms)


def solution(mesh):
    devices = mesh.devices
    mesh = Mesh(devices.reshape(devices.shape[0], -1, 2), ("row",) + COL)
    return jax.shard_map(
        local,
        mesh=mesh,
        in_specs=(
            P(COL, "row"),
            P(),
            P(),
            P(None, "row"),
            P(None, "row"),
            P(None, "row"),
            P("row", None),
            P(None, "row"),
            P(None, "row"),
            P("row", None),
            P(COL, "row", None, None),
            P(COL, "row", None),
            P(COL, None),
            P(COL),
            P(COL, None),
            P(COL),
        ),
        out_specs=(P(COL, "row"), P(COL, "row", None, None), P(COL, "row", None)),
        check_vma=False,
    )
```

```python
import numpy as np

import jax
import jax.numpy as jnp
from jax import lax
from jax.experimental import pallas as pl
from jax.experimental.pallas import tpu as pltpu
from jax.sharding import Mesh, PartitionSpec as P

EPS = 1e-05
COL = ("chip", "core")
FD = 16
F = 1 + FD + FD * FD
PAIRS = [(a, b) for a in range(FD) for b in range(a, FD)]
NFOLD = 1 + FD + len(PAIRS)
RFOLD = 160
LIN = float(FD) ** (-0.25)
QUAD = (2.0 * FD) ** (-0.5)
BF = jnp.bfloat16
F32 = jnp.float32
HI = lax.Precision.HIGHEST
VMEM = pl.BlockSpec(memory_space=pltpu.VMEM)
SMEM = pl.BlockSpec(memory_space=pltpu.SMEM)
ANY = pl.BlockSpec(memory_space=pl.ANY)
PARAMS = pltpu.CompilerParams(vmem_limit_bytes=55 * 1024 * 1024)


def fold_tables():
    first = np.zeros((RFOLD, FD), np.float32)
    second = np.zeros((RFOLD, FD), np.float32)
    fold = np.zeros((RFOLD, F), np.float32)
    fold[0, 0] = 1
    for a in range(FD):
        first[1 + a, a] = 1
        fold[1 + a, 1 + a] = 1
    for p, (a, b) in enumerate(PAIRS):
        row = 1 + FD + p
        first[row, a] = 1
        second[row, b] = 1
        fold[row, 1 + FD + FD * a + b] = 1
        fold[row, 1 + FD + FD * b + a] = 1
    return first, second, fold


def full_tables(copies, rows):
    first = np.zeros((rows, FD), np.float32)
    second = np.zeros((rows, FD), np.float32)
    for f in range(F):
        for c in range(copies):
            row = f * copies + c
            if 1 <= f <= FD:
                first[row, f - 1] = 1
            elif f > FD:
                first[row, (f - 1 - FD) // FD] = 1
                second[row, (f - 1 - FD) % FD] = 1
    return first, second


def dot(a, b, ca, cb, precision=None):
    return lax.dot_general(
        a, b, (((ca,), (cb,)), ((), ())), precision=precision, preferred_element_type=F32
    )


def iota(shape, dim):
    return lax.broadcasted_iota(jnp.int32, shape, dim)


def features(first, second, vec, shift, live):
    one = dot(first, vec, 1, 0)
    two = dot(second, vec, 1, 0)
    feat = iota(one.shape, 0) >> shift
    one = one + jnp.where(feat == 0, 1.0, 0.0)
    two = two + jnp.where(feat <= FD, 1.0, 0.0)
    scale = jnp.where(feat == 0, 1.0, jnp.where(feat <= FD, LIN, QUAD))
    return one * two * jnp.where(feat < live, scale, 0.0)


def pack_kernel(home, request, states, norms, fold, out, folded, slots):
    n_slots = states.shape[1]
    width = states.shape[2]
    lanes = out.shape[2]
    for f in range(1 + FD):
        folded[f] = states[f]
    for p, (a, b) in enumerate(PAIRS):
        one = states[1 + FD + FD * a + b]
        folded[1 + FD + p] = one if a == b else one + states[1 + FD + FD * b + a]
    folded[NFOLD:RFOLD] = jnp.zeros((RFOLD - NFOLD, n_slots, width), BF)
    block = 16
    side = block * n_slots
    row = iota((side, side), 0)
    turn = jnp.where(
        iota((side, side), 1) == (row % block) * n_slots + row // block, 1.0, 0.0
    ).astype(BF)
    for g in range(RFOLD // block):
        part = folded[g * block : (g + 1) * block].reshape(side, width)
        turned = dot(turn, part, 1, 0).astype(BF)
        slots[:, g * block : (g + 1) * block, 0:width] = turned.reshape(n_slots, block, width)
    spread = jnp.where(
        iota((n_slots, lanes), 1) == width + iota((n_slots, lanes), 0), 1.0, 0.0
    )
    by_lane = dot(spread, norms[:, 0, :], 0, 0, HI)
    norm_lanes = dot(fold[...], by_lane, 1, 1, HI)
    out[...] = jnp.zeros(out.shape, out.dtype)
    lane = iota((RFOLD, lanes), 1)
    for s in range(n_slots):
        owner = home[s] * 2 + request[s]
        value = jnp.where(
            lane < width,
            slots[s].astype(F32),
            jnp.where(lane == width + s, norm_lanes, 0.0),
        )
        out[owner] = out[owner] + value.astype(BF)


def gain_columns(gain):
    n = gain.shape[0]
    padded = jnp.concatenate([gain[...], jnp.zeros((16 - n, 128), F32)], axis=0)
    return jnp.transpose(jnp.concatenate([padded] * 8, axis=0))


def normed_columns(load, n, gain):
    cols = gain_columns(gain)
    total = jnp.zeros((1, 128), F32)
    for j in range(n):
        block = load(j)
        total = total + jnp.sum(block * block, axis=0, keepdims=True)
    scale = lax.rsqrt(total / (n * 128) + EPS)
    return [
        (load(j) * scale * cols[:, j : j + 1]).astype(BF) for j in range(n)
    ]


def mix_kernel(accepted, got, hidden, gain, w_q, w_k, w_v, parents, first, second,
               mixed, keys, vals, path):
    n = gain.shape[0]
    width = w_v.shape[0]
    tok = hidden.shape[1]
    half = tok // 2
    row = iota((tok, tok), 0)
    col = iota((tok, tok), 1)
    up = jnp.concatenate([parents[0:1], parents[1:2] + half], axis=1)
    reach = jnp.where((row == up) | (row == col), 1.0, 0.0)
    for repeat in range(6):
        low = reach.astype(BF)
        reach = jnp.minimum(dot(low, low, 1, 0), 1.0)
    normed = jnp.concatenate(
        normed_columns(
            lambda j: hidden[j * 128 : (j + 1) * 128].astype(F32), n, gain
        ),
        axis=0,
    )
    q = dot(w_q[...], normed, 1, 0).astype(BF)
    k = dot(w_k[...], normed, 1, 0).astype(BF)
    v = dot(w_v[...], normed, 1, 0).astype(BF)
    keys[...] = k
    vals[...] = v
    lane8 = iota((8, tok), 1)
    sub8 = iota((8, tok), 0)
    chosen = jnp.where(sub8 == 0, accepted[0], accepted[1] + half)
    pick = jnp.where((lane8 == chosen) & (sub8 < 2), 1.0, 0.0).astype(BF)
    path[...] = dot(pick, reach.astype(BF), 1, 1)
    scaled = dot(k, q, 0, 0) * (1.0 / FD**0.5)
    kernel = (1.0 + scaled + 0.5 * scaled * scaled) * reach
    tree_den = jnp.sum(kernel, axis=0, keepdims=True)
    tree_num = dot(v, kernel.astype(BF), 1, 0)
    phi = features(first[...], second[...], q, 0, NFOLD)
    high_phi = phi.astype(BF)
    low_phi = (phi - high_phi.astype(F32)).astype(BF)
    nums = []
    dens = []
    for r in range(2):
        whole = got[r].astype(F32)
        for i in range(1, got.shape[0] // 2):
            whole = whole + got[2 * i + r].astype(F32)
        high = whole.astype(BF)
        low = (whole - high.astype(F32)).astype(BF)
        both = dot(high, high_phi, 0, 0) + dot(low, high_phi, 0, 0)
        extra = dot(high, low_phi, 0, 0)
        nums.append(both[:width])
        dens.append(jnp.sum(both[width:] + extra[width:], axis=0, keepdims=True))
    lane = iota(nums[0].shape, 1)
    num = jnp.where(lane < half, nums[0], nums[1])
    den = jnp.where(lane[0:1] < half, dens[0], dens[1])
    mixed[...] = ((num + tree_num) / (den + tree_den)).astype(BF)


def page_kernel(keys, vals, path, first2, second2, first1, second1, states, norms):
    k = keys[...]
    phi = features(first2[...], second2[...], k, 1, F)
    mask = jnp.where(iota(phi.shape, 0) % 2 == 0, path[0:1], path[1:2])
    weighted = phi.astype(BF) * mask.astype(BF)
    states[...] = dot(weighted, vals[...], 1, 1).astype(BF)
    phi1 = features(first1[...], second1[...], k, 0, F)
    norms[...] = dot(path[...], phi1, 1, 1, HI)


def mlp_kernel(row_ref, w_out_far, w_gate_far, w_up_far, w_down_far, mixed, hidden, gain,
               down, residual_own, residual, attn, w_out, w_gate, w_up, w_down, sems):
    n = gain.shape[0]
    parts = sems.shape[0] - 3
    size = w_out.shape[0] // parts
    spans = [pl.ds(c * size, size) for c in range(parts)]
    copies = [
        pltpu.make_async_copy(w_out_far.at[span], w_out.at[span], sems.at[c])
        for c, span in enumerate(spans)
    ] + [
        pltpu.make_async_copy(far, near, sems.at[parts + i])
        for i, (far, near) in enumerate(
            ((w_gate_far, w_gate), (w_up_far, w_up), (w_down_far, w_down))
        )
    ]
    for copy in copies:
        copy.start()
    cols = gain_columns(gain)
    for c, span in enumerate(spans):
        copies[c].wait()
        part = dot(mixed[span], w_out[span], 0, 0)
        if c == 0:
            attn[...] = part
        else:
            attn[...] += part
    total = jnp.zeros((1, 128), F32)
    for j in range(n):
        rows = slice(j * 128, (j + 1) * 128)
        block = hidden[rows].astype(F32) + attn[:, rows].T
        residual[rows] = block
        total = total + jnp.sum(block * block, axis=0, keepdims=True)
    own = residual_own.shape[0]
    residual_own[...] = residual[pl.ds(pl.multiple_of(row_ref[0] * own, 8), own)]
    scale = lax.rsqrt(total / (n * 128) + EPS)
    normed = jnp.concatenate(
        [
            (residual[j * 128 : (j + 1) * 128] * scale * cols[:, j : j + 1]).astype(BF)
            for j in range(n)
        ],
        axis=0,
    )
    copies[parts].wait()
    gate = dot(w_gate[...], normed, 1, 0)
    copies[parts + 1].wait()
    up = dot(w_up[...], normed, 1, 0)
    active = (gate / (1.0 + jnp.exp(-gate)) * up).astype(BF)
    copies[parts + 2].wait()
    down[...] = dot(w_down[...], active, 0, 0).astype(BF)


def last_kernel(parts, residual_own, out):
    total = residual_own[...]
    for g in range(parts.shape[0]):
        total = total + parts[g].astype(F32)
    out[...] = total.astype(BF)


def call(kernel, n_smem, args, outs, scratch=(), **extra):
    return pl.pallas_call(
        kernel,
        out_shape=outs,
        in_specs=[SMEM] * n_smem + [VMEM] * (len(args) - n_smem),
        out_specs=jax.tree.map(lambda _: VMEM, outs),
        scratch_shapes=scratch,
        compiler_params=PARAMS,
        **extra,
    )(*args)


def in_vmem(x):
    return pltpu.with_memory_space_constraint(x, pltpu.VMEM)


def shape(dims, dtype):
    return jax.ShapeDtypeStruct(dims, dtype)


def local(
    hidden_in,
    attn_gain,
    mlp_gain,
    w_query,
    w_key,
    w_value,
    w_out,
    w_gate,
    w_up,
    w_down,
    page_states,
    page_norms,
    page_home,
    page_request,
    parents,
    accepted,
):
    n_row = lax.axis_size("row")
    n_col = lax.axis_size(COL)
    tok, own = hidden_in.shape
    width = n_row * own
    value_width = w_value.shape[1]
    slot_count = page_states.shape[0]
    row = lax.axis_index("row").astype(jnp.int32).reshape(1)
    first, second, fold = fold_tables()
    first1, second1 = full_tables(1, 280)
    first2, second2 = full_tables(2, 560)
    first, second, first1, second1, first2, second2 = (
        jnp.asarray(t, BF) for t in (first, second, first1, second1, first2, second2)
    )

    half = w_out.shape[0] // 2
    half_out = lax.dynamic_slice_in_dim(w_out, lax.axis_index("core") * half, half, 0)
    all_out = lax.all_gather(half_out, ("row", "core"), axis=0, tiled=True)

    packed = call(
        pack_kernel,
        2,
        (
            page_home.reshape(slot_count),
            page_request,
            jnp.transpose(page_states[:, 0], (1, 0, 2)),
            page_norms,
            jnp.asarray(fold, F32),
        ),
        shape((2 * n_col, RFOLD, 128), BF),
        (
            pltpu.VMEM((RFOLD, slot_count, value_width), BF),
            pltpu.VMEM((slot_count, RFOLD, 128), BF),
        ),
    )
    packed, hidden_t = lax.optimization_barrier((packed, hidden_in.T))
    got = lax.all_to_all(packed, COL, split_axis=0, concat_axis=0, tiled=True)
    hidden = in_vmem(lax.all_gather(hidden_t, "row", axis=0, tiled=True))

    mixed_own, keys, vals, path = pl.pallas_call(
        mix_kernel,
        out_shape=(
            shape((value_width, tok), BF),
            shape((FD, tok), BF),
            shape((value_width, tok), BF),
            shape((8, tok), F32),
        ),
        in_specs=[SMEM] + [VMEM] * 9,
        out_specs=(VMEM,) * 4,
        compiler_params=PARAMS,
    )(
        accepted,
        in_vmem(got),
        hidden,
        attn_gain.reshape(-1, 128),
        w_query.T,
        w_key.T,
        w_value.T,
        parents,
        first,
        second,
    )

    mixed = in_vmem(lax.all_gather(mixed_own, "row", axis=0, tiled=True))

    states, norms = call(
        page_kernel,
        0,
        (keys, vals, path, first2, second2, first1, second1),
        (shape((560, value_width), BF), shape((8, 280), F32)),
    )

    down, residual_own = pl.pallas_call(
        mlp_kernel,
        out_shape=(shape((width, tok), BF), shape((own, tok), F32)),
        in_specs=[SMEM] + [ANY] * 4 + [VMEM] * 3,
        out_specs=(VMEM,) * 2,
        scratch_shapes=(
            pltpu.VMEM((width, tok), F32),
            pltpu.VMEM((tok, width), F32),
            pltpu.VMEM((width, width), BF),
            pltpu.VMEM(w_gate.shape[::-1], BF),
            pltpu.VMEM(w_up.shape[::-1], BF),
            pltpu.VMEM(w_down.shape, BF),
            pltpu.SemaphoreType.DMA((10,)),
        ),
        compiler_params=PARAMS,
    )(
        row,
        all_out,
        w_gate.T,
        w_up.T,
        w_down,
        mixed,
        hidden,
        mlp_gain.reshape(-1, 128),
    )
    parts = lax.all_to_all(
        down.reshape(n_row, own, tok), "row", split_axis=0, concat_axis=0, tiled=True
    )
    hidden_out = call(last_kernel, 0, (in_vmem(parts), residual_own), shape((own, tok), BF)).T
    new_states = jnp.transpose(states[: 2 * F].reshape(F, 2, value_width), (1, 0, 2))[:, None]
    new_norms = norms[:2, :F][:, None]
    return (hidden_out, new_states, new_norms)


def solution(mesh):
    devices = mesh.devices
    mesh = Mesh(devices.reshape(devices.shape[0], -1, 2), ("row",) + COL)
    return jax.shard_map(
        local,
        mesh=mesh,
        in_specs=(
            P(COL, "row"),
            P(),
            P(),
            P(None, "row"),
            P(None, "row"),
            P(None, "row"),
            P("row", None),
            P(None, "row"),
            P(None, "row"),
            P("row", None),
            P(COL, "row", None, None),
            P(COL, "row", None),
            P(COL, None),
            P(COL),
            P(COL, None),
            P(COL),
        ),
        out_specs=(P(COL, "row"), P(COL, "row", None, None), P(COL, "row", None)),
        check_vma=False,
    )
```

```python
import numpy as np

import jax
import jax.numpy as jnp
from jax import lax
from jax.experimental import pallas as pl
from jax.experimental.pallas import tpu as pltpu
from jax.sharding import Mesh, PartitionSpec as P

EPS = 1e-05
COL = ("chip", "core")
FD = 16
F = 1 + FD + FD * FD
PAIRS = [(a, b) for a in range(FD) for b in range(a, FD)]
NFOLD = 1 + FD + len(PAIRS)
RFOLD = 160
LIN = float(FD) ** (-0.25)
QUAD = (2.0 * FD) ** (-0.5)
BF = jnp.bfloat16
F32 = jnp.float32
HI = lax.Precision.HIGHEST
VMEM = pl.BlockSpec(memory_space=pltpu.VMEM)
SMEM = pl.BlockSpec(memory_space=pltpu.SMEM)
ANY = pl.BlockSpec(memory_space=pl.ANY)
PARAMS = pltpu.CompilerParams(vmem_limit_bytes=55 * 1024 * 1024)


def fold_tables():
    first = np.zeros((RFOLD, FD), np.float32)
    second = np.zeros((RFOLD, FD), np.float32)
    fold = np.zeros((RFOLD, F), np.float32)
    fold[0, 0] = 1
    for a in range(FD):
        first[1 + a, a] = 1
        fold[1 + a, 1 + a] = 1
    for p, (a, b) in enumerate(PAIRS):
        row = 1 + FD + p
        first[row, a] = 1
        second[row, b] = 1
        fold[row, 1 + FD + FD * a + b] = 1
        fold[row, 1 + FD + FD * b + a] = 1
    return first, second, fold


def full_tables(copies, rows):
    first = np.zeros((rows, FD), np.float32)
    second = np.zeros((rows, FD), np.float32)
    for f in range(F):
        for c in range(copies):
            row = f * copies + c
            if 1 <= f <= FD:
                first[row, f - 1] = 1
            elif f > FD:
                first[row, (f - 1 - FD) // FD] = 1
                second[row, (f - 1 - FD) % FD] = 1
    return first, second


def dot(a, b, ca, cb, precision=None):
    return lax.dot_general(
        a, b, (((ca,), (cb,)), ((), ())), precision=precision, preferred_element_type=F32
    )


def iota(shape, dim):
    return lax.broadcasted_iota(jnp.int32, shape, dim)


def features(first, second, vec, shift, live):
    one = dot(first, vec, 1, 0)
    two = dot(second, vec, 1, 0)
    feat = iota(one.shape, 0) >> shift
    one = one + jnp.where(feat == 0, 1.0, 0.0)
    two = two + jnp.where(feat <= FD, 1.0, 0.0)
    scale = jnp.where(feat == 0, 1.0, jnp.where(feat <= FD, LIN, QUAD))
    return one * two * jnp.where(feat < live, scale, 0.0)


def pack_kernel(home, request, states_far, norms, fold, out, states, folded, slots, blank, sems):
    n_slots = states.shape[1]
    width = states.shape[2]
    lanes = out.shape[2]
    clear = blank.shape[0]
    clears = out.shape[0] // clear
    fetch = pltpu.make_async_copy(states_far, states, sems.at[0])
    fetch.start()
    blank[...] = jnp.zeros(blank.shape, BF)
    wipes = [
        pltpu.make_async_copy(blank, out.at[pl.ds(c * clear, clear)], sems.at[1 + c])
        for c in range(clears)
    ]
    for wipe in wipes:
        wipe.start()
    owners = [home[s] * 2 + request[s] for s in range(n_slots)]
    firsts = []
    for s in range(n_slots):
        at = jnp.int32(s)
        for t in range(s - 1, -1, -1):
            at = jnp.where(owners[t] == owners[s], t, at)
        firsts.append(at)
    spread = jnp.where(
        iota((n_slots, lanes), 1) == width + iota((n_slots, lanes), 0), 1.0, 0.0
    )
    by_lane = dot(spread, norms[:, 0, :], 0, 0, HI)
    norm_lanes = dot(fold[...], by_lane, 1, 1, HI)
    block = 16
    side = block * n_slots
    row = iota((side, side), 0)
    turn = jnp.where(
        iota((side, side), 1) == (row % block) * n_slots + row // block, 1.0, 0.0
    ).astype(BF)
    fetch.wait()
    for f in range(1 + FD):
        folded[f] = states[f]
    for p, (a, b) in enumerate(PAIRS):
        one = states[1 + FD + FD * a + b]
        folded[1 + FD + p] = one if a == b else one + states[1 + FD + FD * b + a]
    folded[NFOLD:RFOLD] = jnp.zeros((RFOLD - NFOLD, n_slots, width), BF)
    for g in range(RFOLD // block):
        part = folded[g * block : (g + 1) * block].reshape(side, width)
        turned = dot(turn, part, 1, 0).astype(BF)
        slots[:, g * block : (g + 1) * block, 0:width] = turned.reshape(n_slots, block, width)
    lane = iota((RFOLD, lanes), 1)
    for s in range(n_slots):
        value = jnp.where(
            lane < width,
            slots[s].astype(F32),
            jnp.where(lane == width + s, norm_lanes, 0.0),
        )
        slots[s] = value.astype(BF)
    for s in range(1, n_slots):

        @pl.when(firsts[s] != s)
        def _():
            slots[firsts[s]] = slots[firsts[s]] + slots[s]

    for wipe in wipes:
        wipe.wait()
    for s in range(n_slots):

        @pl.when(firsts[s] == s)
        def _():
            pltpu.make_async_copy(
                slots.at[s], out.at[owners[s]], sems.at[1 + clears + s]
            ).start()

    for s in range(n_slots):

        @pl.when(firsts[s] == s)
        def _():
            pltpu.make_async_copy(
                slots.at[s], out.at[owners[s]], sems.at[1 + clears + s]
            ).wait()


def gain_columns(gain):
    n = gain.shape[0]
    padded = jnp.concatenate([gain[...], jnp.zeros((16 - n, 128), F32)], axis=0)
    return jnp.transpose(jnp.concatenate([padded] * 8, axis=0))


def normed_columns(load, n, gain):
    cols = gain_columns(gain)
    total = jnp.zeros((1, 128), F32)
    for j in range(n):
        block = load(j)
        total = total + jnp.sum(block * block, axis=0, keepdims=True)
    scale = lax.rsqrt(total / (n * 128) + EPS)
    return [
        (load(j) * scale * cols[:, j : j + 1]).astype(BF) for j in range(n)
    ]


def mix_kernel(accepted, got, hidden, gain, w_q, w_k, w_v, parents, first, second,
               mixed, keys, vals, path):
    n = gain.shape[0]
    width = w_v.shape[0]
    tok = hidden.shape[1]
    half = tok // 2
    row = iota((tok, tok), 0)
    col = iota((tok, tok), 1)
    up = jnp.concatenate([parents[0:1], parents[1:2] + half], axis=1)
    reach = jnp.where((row == up) | (row == col), 1.0, 0.0)
    for repeat in range(6):
        low = reach.astype(BF)
        reach = jnp.minimum(dot(low, low, 1, 0), 1.0)
    normed = jnp.concatenate(
        normed_columns(
            lambda j: hidden[j * 128 : (j + 1) * 128].astype(F32), n, gain
        ),
        axis=0,
    )
    q = dot(w_q[...], normed, 1, 0).astype(BF)
    k = dot(w_k[...], normed, 1, 0).astype(BF)
    v = dot(w_v[...], normed, 1, 0).astype(BF)
    keys[...] = k
    vals[...] = v
    lane8 = iota((8, tok), 1)
    sub8 = iota((8, tok), 0)
    chosen = jnp.where(sub8 == 0, accepted[0], accepted[1] + half)
    pick = jnp.where((lane8 == chosen) & (sub8 < 2), 1.0, 0.0).astype(BF)
    path[...] = dot(pick, reach.astype(BF), 1, 1)
    scaled = dot(k, q, 0, 0) * (1.0 / FD**0.5)
    kernel = (1.0 + scaled + 0.5 * scaled * scaled) * reach
    tree_den = jnp.sum(kernel, axis=0, keepdims=True)
    tree_num = dot(v, kernel.astype(BF), 1, 0)
    phi = features(first[...], second[...], q, 0, NFOLD)
    high_phi = phi.astype(BF)
    low_phi = (phi - high_phi.astype(F32)).astype(BF)
    nums = []
    dens = []
    for r in range(2):
        whole = got[r].astype(F32)
        for i in range(1, got.shape[0] // 2):
            whole = whole + got[2 * i + r].astype(F32)
        high = whole.astype(BF)
        low = (whole - high.astype(F32)).astype(BF)
        both = dot(high, high_phi, 0, 0) + dot(low, high_phi, 0, 0)
        extra = dot(high, low_phi, 0, 0)
        nums.append(both[:width])
        dens.append(jnp.sum(both[width:] + extra[width:], axis=0, keepdims=True))
    lane = iota(nums[0].shape, 1)
    num = jnp.where(lane < half, nums[0], nums[1])
    den = jnp.where(lane[0:1] < half, dens[0], dens[1])
    mixed[...] = ((num + tree_num) / (den + tree_den)).astype(BF)


def page_kernel(keys, vals, path, first2, second2, first1, second1, states, norms):
    k = keys[...]
    phi = features(first2[...], second2[...], k, 1, F)
    mask = jnp.where(iota(phi.shape, 0) % 2 == 0, path[0:1], path[1:2])
    weighted = phi.astype(BF) * mask.astype(BF)
    states[...] = dot(weighted, vals[...], 1, 1).astype(BF)
    phi1 = features(first1[...], second1[...], k, 0, F)
    norms[...] = dot(path[...], phi1, 1, 1, HI)


def mlp_kernel(row_ref, w_out_far, w_gate_far, w_up_far, w_down_far, mixed, hidden, gain,
               down, residual_own, residual, attn, w_out, w_gate, w_up, w_down, sems):
    n = gain.shape[0]
    parts = sems.shape[0] - 3
    size = w_out.shape[0] // parts
    spans = [pl.ds(c * size, size) for c in range(parts)]
    copies = [
        pltpu.make_async_copy(w_out_far.at[span], w_out.at[span], sems.at[c])
        for c, span in enumerate(spans)
    ] + [
        pltpu.make_async_copy(far, near, sems.at[parts + i])
        for i, (far, near) in enumerate(
            ((w_gate_far, w_gate), (w_up_far, w_up), (w_down_far, w_down))
        )
    ]
    for copy in copies:
        copy.start()
    cols = gain_columns(gain)
    for c, span in enumerate(spans):
        copies[c].wait()
        part = dot(mixed[span], w_out[span], 0, 0)
        if c == 0:
            attn[...] = part
        else:
            attn[...] += part
    total = jnp.zeros((1, 128), F32)
    for j in range(n):
        rows = slice(j * 128, (j + 1) * 128)
        block = hidden[rows].astype(F32) + attn[:, rows].T
        residual[rows] = block
        total = total + jnp.sum(block * block, axis=0, keepdims=True)
    own = residual_own.shape[0]
    residual_own[...] = residual[pl.ds(pl.multiple_of(row_ref[0] * own, 8), own)]
    scale = lax.rsqrt(total / (n * 128) + EPS)
    normed = jnp.concatenate(
        [
            (residual[j * 128 : (j + 1) * 128] * scale * cols[:, j : j + 1]).astype(BF)
            for j in range(n)
        ],
        axis=0,
    )
    copies[parts].wait()
    gate = dot(w_gate[...], normed, 1, 0)
    copies[parts + 1].wait()
    up = dot(w_up[...], normed, 1, 0)
    active = (gate / (1.0 + jnp.exp(-gate)) * up).astype(BF)
    copies[parts + 2].wait()
    down[...] = dot(w_down[...], active, 0, 0).astype(BF)


def last_kernel(parts, residual_own, out):
    total = residual_own[...]
    for g in range(parts.shape[0]):
        total = total + parts[g].astype(F32)
    out[...] = total.astype(BF)


def call(kernel, n_smem, args, outs, scratch=(), **extra):
    return pl.pallas_call(
        kernel,
        out_shape=outs,
        in_specs=[SMEM] * n_smem + [VMEM] * (len(args) - n_smem),
        out_specs=jax.tree.map(lambda _: VMEM, outs),
        scratch_shapes=scratch,
        compiler_params=PARAMS,
        **extra,
    )(*args)


def in_vmem(x):
    return pltpu.with_memory_space_constraint(x, pltpu.VMEM)


def shape(dims, dtype):
    return jax.ShapeDtypeStruct(dims, dtype)


def local(
    hidden_in,
    attn_gain,
    mlp_gain,
    w_query,
    w_key,
    w_value,
    w_out,
    w_gate,
    w_up,
    w_down,
    page_states,
    page_norms,
    page_home,
    page_request,
    parents,
    accepted,
):
    n_row = lax.axis_size("row")
    n_col = lax.axis_size(COL)
    tok, own = hidden_in.shape
    width = n_row * own
    value_width = w_value.shape[1]
    slot_count = page_states.shape[0]
    row = lax.axis_index("row").astype(jnp.int32).reshape(1)
    first, second, fold = fold_tables()
    first1, second1 = full_tables(1, 280)
    first2, second2 = full_tables(2, 560)
    first, second, first1, second1, first2, second2 = (
        jnp.asarray(t, BF) for t in (first, second, first1, second1, first2, second2)
    )

    half = w_out.shape[0] // 2
    half_out = lax.dynamic_slice_in_dim(w_out, lax.axis_index("core") * half, half, 0)
    all_out = lax.all_gather(half_out, ("row", "core"), axis=0, tiled=True)

    packed = pl.pallas_call(
        pack_kernel,
        out_shape=shape((2 * n_col, RFOLD, 128), BF),
        in_specs=[SMEM] * 2 + [ANY] + [VMEM] * 2,
        out_specs=ANY,
        scratch_shapes=(
            pltpu.VMEM((F, slot_count, value_width), BF),
            pltpu.VMEM((RFOLD, slot_count, value_width), BF),
            pltpu.VMEM((slot_count, RFOLD, 128), BF),
            pltpu.VMEM((8, RFOLD, 128), BF),
            pltpu.SemaphoreType.DMA((1 + 2 * n_col // 8 + slot_count,)),
        ),
        compiler_params=PARAMS,
    )(
        page_home.reshape(slot_count),
        page_request,
        jnp.transpose(page_states[:, 0], (1, 0, 2)),
        page_norms,
        jnp.asarray(fold, F32),
    )
    packed, hidden_t = lax.optimization_barrier((packed, hidden_in.T))
    got = lax.all_to_all(packed, COL, split_axis=0, concat_axis=0, tiled=True)
    hidden = in_vmem(lax.all_gather(hidden_t, "row", axis=0, tiled=True))

    mixed_own, keys, vals, path = pl.pallas_call(
        mix_kernel,
        out_shape=(
            shape((value_width, tok), BF),
            shape((FD, tok), BF),
            shape((value_width, tok), BF),
            shape((8, tok), F32),
        ),
        in_specs=[SMEM] + [VMEM] * 9,
        out_specs=(VMEM,) * 4,
        compiler_params=PARAMS,
    )(
        accepted,
        in_vmem(got),
        hidden,
        attn_gain.reshape(-1, 128),
        w_query.T,
        w_key.T,
        w_value.T,
        parents,
        first,
        second,
    )

    mixed = in_vmem(lax.all_gather(mixed_own, "row", axis=0, tiled=True))

    states, norms = call(
        page_kernel,
        0,
        (keys, vals, path, first2, second2, first1, second1),
        (shape((560, value_width), BF), shape((8, 280), F32)),
    )

    down, residual_own = pl.pallas_call(
        mlp_kernel,
        out_shape=(pltpu.VMEM((width, tok), BF), pltpu.VMEM((own, tok), F32)),
        in_specs=[SMEM] + [ANY] * 4 + [VMEM] * 3,
        out_specs=(VMEM,) * 2,
        scratch_shapes=(
            pltpu.VMEM((width, tok), F32),
            pltpu.VMEM((tok, width), F32),
            pltpu.VMEM((width, width), BF),
            pltpu.VMEM(w_gate.shape[::-1], BF),
            pltpu.VMEM(w_up.shape[::-1], BF),
            pltpu.VMEM(w_down.shape, BF),
            pltpu.SemaphoreType.DMA((10,)),
        ),
        compiler_params=PARAMS,
    )(
        row,
        all_out,
        w_gate.T,
        w_up.T,
        w_down,
        mixed,
        hidden,
        mlp_gain.reshape(-1, 128),
    )
    parts = lax.all_to_all(
        down.reshape(n_row, own, tok), "row", split_axis=0, concat_axis=0, tiled=True
    )
    hidden_out = call(last_kernel, 0, (in_vmem(parts), in_vmem(residual_own)), shape((own, tok), BF)).T
    new_states = jnp.transpose(states[: 2 * F].reshape(F, 2, value_width), (1, 0, 2))[:, None]
    new_norms = norms[:2, :F][:, None]
    return (hidden_out, new_states, new_norms)


def solution(mesh):
    devices = mesh.devices
    mesh = Mesh(devices.reshape(devices.shape[0], -1, 2), ("row",) + COL)
    return jax.shard_map(
        local,
        mesh=mesh,
        in_specs=(
            P(COL, "row"),
            P(),
            P(),
            P(None, "row"),
            P(None, "row"),
            P(None, "row"),
            P("row", None),
            P(None, "row"),
            P(None, "row"),
            P("row", None),
            P(COL, "row", None, None),
            P(COL, "row", None),
            P(COL, None),
            P(COL),
            P(COL, None),
            P(COL),
        ),
        out_specs=(P(COL, "row"), P(COL, "row", None, None), P(COL, "row", None)),
        check_vma=False,
    )
```

```python
import numpy as np

import jax
import jax.numpy as jnp
from jax import lax
from jax.experimental import pallas as pl
from jax.experimental.pallas import tpu as pltpu
from jax.sharding import Mesh, PartitionSpec as P

EPS = 1e-05
COL = ("chip", "core")
FD = 16
F = 1 + FD + FD * FD
PAIRS = [(a, b) for a in range(FD) for b in range(a, FD)]
NFOLD = 1 + FD + len(PAIRS)
RFOLD = 160
LIN = float(FD) ** (-0.25)
QUAD = (2.0 * FD) ** (-0.5)
BF = jnp.bfloat16
F32 = jnp.float32
HI = lax.Precision.HIGHEST
VMEM = pl.BlockSpec(memory_space=pltpu.VMEM)
SMEM = pl.BlockSpec(memory_space=pltpu.SMEM)
ANY = pl.BlockSpec(memory_space=pl.ANY)
PARAMS = pltpu.CompilerParams(vmem_limit_bytes=55 * 1024 * 1024)


def fold_tables():
    first = np.zeros((RFOLD, FD), np.float32)
    second = np.zeros((RFOLD, FD), np.float32)
    fold = np.zeros((RFOLD, F), np.float32)
    fold[0, 0] = 1
    for a in range(FD):
        first[1 + a, a] = 1
        fold[1 + a, 1 + a] = 1
    for p, (a, b) in enumerate(PAIRS):
        row = 1 + FD + p
        first[row, a] = 1
        second[row, b] = 1
        fold[row, 1 + FD + FD * a + b] = 1
        fold[row, 1 + FD + FD * b + a] = 1
    return first, second, fold


def full_tables(copies, rows):
    first = np.zeros((rows, FD), np.float32)
    second = np.zeros((rows, FD), np.float32)
    for f in range(F):
        for c in range(copies):
            row = f * copies + c
            if 1 <= f <= FD:
                first[row, f - 1] = 1
            elif f > FD:
                first[row, (f - 1 - FD) // FD] = 1
                second[row, (f - 1 - FD) % FD] = 1
    return first, second


def dot(a, b, ca, cb, precision=None):
    return lax.dot_general(
        a, b, (((ca,), (cb,)), ((), ())), precision=precision, preferred_element_type=F32
    )


def iota(shape, dim):
    return lax.broadcasted_iota(jnp.int32, shape, dim)


def features(first, second, vec, shift, live):
    one = dot(first, vec, 1, 0)
    two = dot(second, vec, 1, 0)
    feat = iota(one.shape, 0) >> shift
    one = one + jnp.where(feat == 0, 1.0, 0.0)
    two = two + jnp.where(feat <= FD, 1.0, 0.0)
    scale = jnp.where(feat == 0, 1.0, jnp.where(feat <= FD, LIN, QUAD))
    return one * two * jnp.where(feat < live, scale, 0.0)


def pack_kernel(home, request, states_far, norms, fold, out, states, folded, slots, blank, sems):
    n_slots = states.shape[1]
    width = states.shape[2]
    lanes = out.shape[2]
    clear = blank.shape[0]
    clears = out.shape[0] // clear
    fetch = pltpu.make_async_copy(states_far, states, sems.at[0])
    fetch.start()
    blank[...] = jnp.zeros(blank.shape, BF)
    wipes = [
        pltpu.make_async_copy(blank, out.at[pl.ds(c * clear, clear)], sems.at[1 + c])
        for c in range(clears)
    ]
    for wipe in wipes:
        wipe.start()
    owners = [home[s] * 2 + request[s] for s in range(n_slots)]
    firsts = []
    for s in range(n_slots):
        at = jnp.int32(s)
        for t in range(s - 1, -1, -1):
            at = jnp.where(owners[t] == owners[s], t, at)
        firsts.append(at)
    spread = jnp.where(
        iota((n_slots, lanes), 1) == width + iota((n_slots, lanes), 0), 1.0, 0.0
    )
    by_lane = dot(spread, norms[:, 0, :], 0, 0, HI)
    norm_lanes = dot(fold[...], by_lane, 1, 1, HI)
    block = 16
    side = block * n_slots
    row = iota((side, side), 0)
    turn = jnp.where(
        iota((side, side), 1) == (row % block) * n_slots + row // block, 1.0, 0.0
    ).astype(BF)
    fetch.wait()
    for f in range(1 + FD):
        folded[f] = states[f]
    for p, (a, b) in enumerate(PAIRS):
        one = states[1 + FD + FD * a + b]
        folded[1 + FD + p] = one if a == b else one + states[1 + FD + FD * b + a]
    folded[NFOLD:RFOLD] = jnp.zeros((RFOLD - NFOLD, n_slots, width), BF)
    for g in range(RFOLD // block):
        part = folded[g * block : (g + 1) * block].reshape(side, width)
        turned = dot(turn, part, 1, 0).astype(BF)
        slots[:, g * block : (g + 1) * block, 0:width] = turned.reshape(n_slots, block, width)
    lane = iota((RFOLD, lanes), 1)
    for s in range(n_slots):
        value = jnp.where(
            lane < width,
            slots[s].astype(F32),
            jnp.where(lane == width + s, norm_lanes, 0.0),
        )
        slots[s] = value.astype(BF)
    for s in range(1, n_slots):

        @pl.when(firsts[s] != s)
        def _():
            slots[firsts[s]] = slots[firsts[s]] + slots[s]

    for wipe in wipes:
        wipe.wait()
    for s in range(n_slots):

        @pl.when(firsts[s] == s)
        def _():
            pltpu.make_async_copy(
                slots.at[s], out.at[owners[s]], sems.at[1 + clears + s]
            ).start()

    for s in range(n_slots):

        @pl.when(firsts[s] == s)
        def _():
            pltpu.make_async_copy(
                slots.at[s], out.at[owners[s]], sems.at[1 + clears + s]
            ).wait()


def gain_columns(gain):
    n = gain.shape[0]
    padded = jnp.concatenate([gain[...], jnp.zeros((16 - n, 128), F32)], axis=0)
    return jnp.transpose(jnp.concatenate([padded] * 8, axis=0))


def normed_columns(load, n, gain):
    cols = gain_columns(gain)
    total = jnp.zeros((1, 128), F32)
    for j in range(n):
        block = load(j)
        total = total + jnp.sum(block * block, axis=0, keepdims=True)
    scale = lax.rsqrt(total / (n * 128) + EPS)
    return [
        (load(j) * scale * cols[:, j : j + 1]).astype(BF) for j in range(n)
    ]


def mix_kernel(accepted, got, hidden, gain, w_q, w_k, w_v, parents, first, second,
               mixed, keys, vals, path):
    n = gain.shape[0]
    width = w_v.shape[0]
    tok = hidden.shape[1]
    half = tok // 2
    row = iota((tok, tok), 0)
    col = iota((tok, tok), 1)
    up = jnp.concatenate([parents[0:1], parents[1:2] + half], axis=1)
    reach = jnp.where((row == up) | (row == col), 1.0, 0.0)
    for repeat in range(6):
        low = reach.astype(BF)
        reach = jnp.minimum(dot(low, low, 1, 0), 1.0)
    normed = jnp.concatenate(
        normed_columns(
            lambda j: hidden[j * 128 : (j + 1) * 128].astype(F32), n, gain
        ),
        axis=0,
    )
    q = dot(w_q[...], normed, 1, 0).astype(BF)
    k = dot(w_k[...], normed, 1, 0).astype(BF)
    v = dot(w_v[...], normed, 1, 0).astype(BF)
    keys[...] = k
    vals[...] = v
    lane8 = iota((8, tok), 1)
    sub8 = iota((8, tok), 0)
    chosen = jnp.where(sub8 == 0, accepted[0], accepted[1] + half)
    pick = jnp.where((lane8 == chosen) & (sub8 < 2), 1.0, 0.0).astype(BF)
    path[...] = dot(pick, reach.astype(BF), 1, 1)
    scaled = dot(k, q, 0, 0) * (1.0 / FD**0.5)
    kernel = (1.0 + scaled + 0.5 * scaled * scaled) * reach
    tree_den = jnp.sum(kernel, axis=0, keepdims=True)
    tree_num = dot(v, kernel.astype(BF), 1, 0)
    phi = features(first[...], second[...], q, 0, NFOLD)
    high_phi = phi.astype(BF)
    low_phi = (phi - high_phi.astype(F32)).astype(BF)
    nums = []
    dens = []
    for r in range(2):
        whole = got[r].astype(F32)
        for i in range(1, got.shape[0] // 2):
            whole = whole + got[2 * i + r].astype(F32)
        high = whole.astype(BF)
        low = (whole - high.astype(F32)).astype(BF)
        both = dot(high, high_phi, 0, 0) + dot(low, high_phi, 0, 0)
        extra = dot(high, low_phi, 0, 0)
        nums.append(both[:width])
        dens.append(jnp.sum(both[width:] + extra[width:], axis=0, keepdims=True))
    lane = iota(nums[0].shape, 1)
    num = jnp.where(lane < half, nums[0], nums[1])
    den = jnp.where(lane[0:1] < half, dens[0], dens[1])
    mixed[...] = ((num + tree_num) / (den + tree_den)).astype(BF)


def page_kernel(keys, vals, path, first2, second2, first1, second1, states, norms):
    k = keys[...]
    phi = features(first2[...], second2[...], k, 1, F)
    mask = jnp.where(iota(phi.shape, 0) % 2 == 0, path[0:1], path[1:2])
    weighted = phi.astype(BF) * mask.astype(BF)
    states[...] = dot(weighted, vals[...], 1, 1).astype(BF)
    phi1 = features(first1[...], second1[...], k, 0, F)
    norms[...] = dot(path[...], phi1, 1, 1, HI)


def mlp_kernel(row_ref, w_out_far, w_gate_far, w_up_far, w_down_far, mixed, hidden, gain,
               down, residual_own, residual, attn, w_out, w_gate, w_up, w_down, sems):
    n = gain.shape[0]
    parts = sems.shape[0] - 3
    size = w_out.shape[0] // parts
    spans = [pl.ds(c * size, size) for c in range(parts)]
    copies = [
        pltpu.make_async_copy(w_out_far.at[span], w_out.at[span], sems.at[c])
        for c, span in enumerate(spans)
    ] + [
        pltpu.make_async_copy(far, near, sems.at[parts + i])
        for i, (far, near) in enumerate(
            ((w_gate_far, w_gate), (w_up_far, w_up), (w_down_far, w_down))
        )
    ]
    for copy in copies:
        copy.start()
    cols = gain_columns(gain)
    for c, span in enumerate(spans):
        copies[c].wait()
        part = dot(mixed[span], w_out[span], 0, 0)
        if c == 0:
            attn[...] = part
        else:
            attn[...] += part
    total = jnp.zeros((1, 128), F32)
    for j in range(n):
        rows = slice(j * 128, (j + 1) * 128)
        block = hidden[rows].astype(F32) + attn[:, rows].T
        residual[rows] = block
        total = total + jnp.sum(block * block, axis=0, keepdims=True)
    own = residual_own.shape[0]
    residual_own[...] = residual[pl.ds(pl.multiple_of(row_ref[0] * own, 8), own)]
    scale = lax.rsqrt(total / (n * 128) + EPS)
    normed = jnp.concatenate(
        [
            (residual[j * 128 : (j + 1) * 128] * scale * cols[:, j : j + 1]).astype(BF)
            for j in range(n)
        ],
        axis=0,
    )
    copies[parts].wait()
    gate = dot(w_gate[...], normed, 1, 0)
    copies[parts + 1].wait()
    up = dot(w_up[...], normed, 1, 0)
    active = (gate / (1.0 + jnp.exp(-gate)) * up).astype(BF)
    copies[parts + 2].wait()
    down[...] = dot(w_down[...], active, 0, 0).astype(BF)


def last_kernel(parts, residual_own, out):
    total = residual_own[...]
    for g in range(parts.shape[0]):
        total = total + parts[g].astype(F32)
    out[...] = total.astype(BF)


def call(kernel, n_smem, args, outs, scratch=(), **extra):
    return pl.pallas_call(
        kernel,
        out_shape=outs,
        in_specs=[SMEM] * n_smem + [VMEM] * (len(args) - n_smem),
        out_specs=jax.tree.map(lambda _: VMEM, outs),
        scratch_shapes=scratch,
        compiler_params=PARAMS,
        **extra,
    )(*args)


def in_vmem(x):
    return pltpu.with_memory_space_constraint(x, pltpu.VMEM)


def shape(dims, dtype):
    return jax.ShapeDtypeStruct(dims, dtype)


def local(
    hidden_in,
    attn_gain,
    mlp_gain,
    w_query,
    w_key,
    w_value,
    w_out,
    w_gate,
    w_up,
    w_down,
    page_states,
    page_norms,
    page_home,
    page_request,
    parents,
    accepted,
):
    n_row = lax.axis_size("row")
    n_col = lax.axis_size(COL)
    tok, own = hidden_in.shape
    width = n_row * own
    value_width = w_value.shape[1]
    slot_count = page_states.shape[0]
    row = lax.axis_index("row").astype(jnp.int32).reshape(1)
    first, second, fold = fold_tables()
    first1, second1 = full_tables(1, 280)
    first2, second2 = full_tables(2, 560)
    first, second, first1, second1, first2, second2 = (
        jnp.asarray(t, BF) for t in (first, second, first1, second1, first2, second2)
    )

    half = w_out.shape[0] // 2
    half_out = lax.dynamic_slice_in_dim(w_out, lax.axis_index("core") * half, half, 0)
    all_out = lax.all_gather(half_out, ("row", "core"), axis=0, tiled=True)

    packed = pl.pallas_call(
        pack_kernel,
        out_shape=shape((2 * n_col, RFOLD, 128), BF),
        in_specs=[SMEM] * 2 + [ANY] + [VMEM] * 2,
        out_specs=ANY,
        scratch_shapes=(
            pltpu.VMEM((F, slot_count, value_width), BF),
            pltpu.VMEM((RFOLD, slot_count, value_width), BF),
            pltpu.VMEM((slot_count, RFOLD, 128), BF),
            pltpu.VMEM((8, RFOLD, 128), BF),
            pltpu.SemaphoreType.DMA((1 + 2 * n_col // 8 + slot_count,)),
        ),
        compiler_params=PARAMS,
    )(
        page_home.reshape(slot_count),
        page_request,
        jnp.transpose(page_states[:, 0], (1, 0, 2)),
        page_norms,
        jnp.asarray(fold, F32),
    )
    packed, hidden_t = lax.optimization_barrier((packed, hidden_in.T))
    got = lax.all_to_all(packed, COL, split_axis=0, concat_axis=0, tiled=True)
    hidden = in_vmem(lax.all_gather(hidden_t, "row", axis=0, tiled=True))

    mixed_own, keys, vals, path = pl.pallas_call(
        mix_kernel,
        out_shape=(
            pltpu.VMEM((value_width, tok), BF),
            shape((FD, tok), BF),
            shape((value_width, tok), BF),
            shape((8, tok), F32),
        ),
        in_specs=[SMEM] + [VMEM] * 9,
        out_specs=(VMEM,) * 4,
        compiler_params=PARAMS,
    )(
        accepted,
        in_vmem(got),
        hidden,
        attn_gain.reshape(-1, 128),
        w_query.T,
        w_key.T,
        w_value.T,
        parents,
        first,
        second,
    )

    mixed = in_vmem(lax.all_gather(mixed_own, "row", axis=0, tiled=True))

    states, norms = call(
        page_kernel,
        0,
        (keys, vals, path, first2, second2, first1, second1),
        (shape((560, value_width), BF), shape((8, 280), F32)),
    )

    down, residual_own = pl.pallas_call(
        mlp_kernel,
        out_shape=(pltpu.VMEM((width, tok), BF), pltpu.VMEM((own, tok), F32)),
        in_specs=[SMEM] + [ANY] * 4 + [VMEM] * 3,
        out_specs=(VMEM,) * 2,
        scratch_shapes=(
            pltpu.VMEM((width, tok), F32),
            pltpu.VMEM((tok, width), F32),
            pltpu.VMEM((width, width), BF),
            pltpu.VMEM(w_gate.shape[::-1], BF),
            pltpu.VMEM(w_up.shape[::-1], BF),
            pltpu.VMEM(w_down.shape, BF),
            pltpu.SemaphoreType.DMA((7,)),
        ),
        compiler_params=PARAMS,
    )(
        row,
        all_out,
        w_gate.T,
        w_up.T,
        w_down,
        mixed,
        hidden,
        mlp_gain.reshape(-1, 128),
    )
    parts = lax.all_to_all(
        down.reshape(n_row, own, tok), "row", split_axis=0, concat_axis=0, tiled=True
    )
    hidden_out = call(last_kernel, 0, (in_vmem(parts), in_vmem(residual_own)), shape((own, tok), BF)).T
    new_states = jnp.transpose(states[: 2 * F].reshape(F, 2, value_width), (1, 0, 2))[:, None]
    new_norms = norms[:2, :F][:, None]
    return (hidden_out, new_states, new_norms)


def solution(mesh):
    devices = mesh.devices
    mesh = Mesh(devices.reshape(devices.shape[0], -1, 2), ("row",) + COL)
    return jax.shard_map(
        local,
        mesh=mesh,
        in_specs=(
            P(COL, "row"),
            P(),
            P(),
            P(None, "row"),
            P(None, "row"),
            P(None, "row"),
            P("row", None),
            P(None, "row"),
            P(None, "row"),
            P("row", None),
            P(COL, "row", None, None),
            P(COL, "row", None),
            P(COL, None),
            P(COL),
            P(COL, None),
            P(COL),
        ),
        out_specs=(P(COL, "row"), P(COL, "row", None, None), P(COL, "row", None)),
        check_vma=False,
    )
```

```python
import numpy as np

import jax
import jax.numpy as jnp
from jax import lax
from jax.experimental import pallas as pl
from jax.experimental.pallas import tpu as pltpu
from jax.sharding import Mesh, PartitionSpec as P

EPS = 1e-05
COL = ("chip", "core")
FD = 16
F = 1 + FD + FD * FD
PAIRS = [(a, b) for a in range(FD) for b in range(a, FD)]
NFOLD = 1 + FD + len(PAIRS)
RFOLD = 160
LIN = float(FD) ** (-0.25)
QUAD = (2.0 * FD) ** (-0.5)
BF = jnp.bfloat16
F32 = jnp.float32
HI = lax.Precision.HIGHEST
VMEM = pl.BlockSpec(memory_space=pltpu.VMEM)
SMEM = pl.BlockSpec(memory_space=pltpu.SMEM)
ANY = pl.BlockSpec(memory_space=pl.ANY)
PARAMS = pltpu.CompilerParams(vmem_limit_bytes=55 * 1024 * 1024)


def fold_tables():
    first = np.zeros((RFOLD, FD), np.float32)
    second = np.zeros((RFOLD, FD), np.float32)
    fold = np.zeros((RFOLD, F), np.float32)
    fold[0, 0] = 1
    for a in range(FD):
        first[1 + a, a] = 1
        fold[1 + a, 1 + a] = 1
    for p, (a, b) in enumerate(PAIRS):
        row = 1 + FD + p
        first[row, a] = 1
        second[row, b] = 1
        fold[row, 1 + FD + FD * a + b] = 1
        fold[row, 1 + FD + FD * b + a] = 1
    return first, second, fold


def full_tables(copies, rows):
    first = np.zeros((rows, FD), np.float32)
    second = np.zeros((rows, FD), np.float32)
    for f in range(F):
        for c in range(copies):
            row = f * copies + c
            if 1 <= f <= FD:
                first[row, f - 1] = 1
            elif f > FD:
                first[row, (f - 1 - FD) // FD] = 1
                second[row, (f - 1 - FD) % FD] = 1
    return first, second


def dot(a, b, ca, cb, precision=None):
    return lax.dot_general(
        a, b, (((ca,), (cb,)), ((), ())), precision=precision, preferred_element_type=F32
    )


def iota(shape, dim):
    return lax.broadcasted_iota(jnp.int32, shape, dim)


def features(first, second, vec, shift, live):
    one = dot(first, vec, 1, 0)
    two = dot(second, vec, 1, 0)
    feat = iota(one.shape, 0) >> shift
    one = one + jnp.where(feat == 0, 1.0, 0.0)
    two = two + jnp.where(feat <= FD, 1.0, 0.0)
    scale = jnp.where(feat == 0, 1.0, jnp.where(feat <= FD, LIN, QUAD))
    return one * two * jnp.where(feat < live, scale, 0.0)


def pack_kernel(home, request, states_far, norms, fold, out, states, folded, slots, blank, sems):
    n_slots = states.shape[1]
    width = states.shape[2]
    lanes = out.shape[2]
    clear = blank.shape[0]
    clears = out.shape[0] // clear
    fetch = pltpu.make_async_copy(states_far, states, sems.at[0])
    fetch.start()
    blank[...] = jnp.zeros(blank.shape, BF)
    wipes = [
        pltpu.make_async_copy(blank, out.at[pl.ds(c * clear, clear)], sems.at[1 + c])
        for c in range(clears)
    ]
    for wipe in wipes:
        wipe.start()
    owners = [home[s] * 2 + request[s] for s in range(n_slots)]
    firsts = []
    for s in range(n_slots):
        at = jnp.int32(s)
        for t in range(s - 1, -1, -1):
            at = jnp.where(owners[t] == owners[s], t, at)
        firsts.append(at)
    spread = jnp.where(
        iota((n_slots, lanes), 1) == width + iota((n_slots, lanes), 0), 1.0, 0.0
    )
    by_lane = dot(spread, norms[:, 0, :], 0, 0, HI)
    norm_lanes = dot(fold[...], by_lane, 1, 1, HI)
    block = 16
    side = block * n_slots
    row = iota((side, side), 0)
    turn = jnp.where(
        iota((side, side), 1) == (row % block) * n_slots + row // block, 1.0, 0.0
    ).astype(BF)
    fetch.wait()
    for f in range(1 + FD):
        folded[f] = states[f]
    for p, (a, b) in enumerate(PAIRS):
        one = states[1 + FD + FD * a + b]
        folded[1 + FD + p] = one if a == b else one + states[1 + FD + FD * b + a]
    folded[NFOLD:RFOLD] = jnp.zeros((RFOLD - NFOLD, n_slots, width), BF)
    for g in range(RFOLD // block):
        part = folded[g * block : (g + 1) * block].reshape(side, width)
        turned = dot(turn, part, 1, 0).astype(BF)
        slots[:, g * block : (g + 1) * block, 0:width] = turned.reshape(n_slots, block, width)
    lane = iota((RFOLD, lanes), 1)
    for s in range(n_slots):
        value = jnp.where(
            lane < width,
            slots[s].astype(F32),
            jnp.where(lane == width + s, norm_lanes, 0.0),
        )
        slots[s] = value.astype(BF)
    for s in range(1, n_slots):

        @pl.when(firsts[s] != s)
        def _():
            slots[firsts[s]] = slots[firsts[s]] + slots[s]

    for wipe in wipes:
        wipe.wait()
    for s in range(n_slots):

        @pl.when(firsts[s] == s)
        def _():
            pltpu.make_async_copy(
                slots.at[s], out.at[owners[s]], sems.at[1 + clears + s]
            ).start()

    for s in range(n_slots):

        @pl.when(firsts[s] == s)
        def _():
            pltpu.make_async_copy(
                slots.at[s], out.at[owners[s]], sems.at[1 + clears + s]
            ).wait()


def gain_columns(gain):
    n = gain.shape[0]
    padded = jnp.concatenate([gain[...], jnp.zeros((16 - n, 128), F32)], axis=0)
    return jnp.transpose(jnp.concatenate([padded] * 8, axis=0))


def normed_columns(load, n, gain):
    cols = gain_columns(gain)
    total = jnp.zeros((1, 128), F32)
    for j in range(n):
        block = load(j)
        total = total + jnp.sum(block * block, axis=0, keepdims=True)
    scale = lax.rsqrt(total / (n * 128) + EPS)
    return [
        (load(j) * scale * cols[:, j : j + 1]).astype(BF) for j in range(n)
    ]


def mix_kernel(accepted, got, hidden, gain, w_q, w_k, w_v, parents, first, second,
               mixed, keys, vals, path):
    n = gain.shape[0]
    width = w_v.shape[0]
    tok = hidden.shape[1]
    half = tok // 2
    row = iota((tok, tok), 0)
    col = iota((tok, tok), 1)
    up = jnp.concatenate([parents[0:1], parents[1:2] + half], axis=1)
    reach = jnp.where((row == up) | (row == col), 1.0, 0.0)
    for repeat in range(6):
        low = reach.astype(BF)
        reach = jnp.minimum(dot(low, low, 1, 0), 1.0)
    normed = jnp.concatenate(
        normed_columns(
            lambda j: hidden[j * 128 : (j + 1) * 128].astype(F32), n, gain
        ),
        axis=0,
    )
    q = dot(w_q[...], normed, 1, 0).astype(BF)
    k = dot(w_k[...], normed, 1, 0).astype(BF)
    v = dot(w_v[...], normed, 1, 0).astype(BF)
    keys[...] = k
    vals[...] = v
    lane8 = iota((8, tok), 1)
    sub8 = iota((8, tok), 0)
    chosen = jnp.where(sub8 == 0, accepted[0], accepted[1] + half)
    pick = jnp.where((lane8 == chosen) & (sub8 < 2), 1.0, 0.0).astype(BF)
    path[...] = dot(pick, reach.astype(BF), 1, 1)
    scaled = dot(k, q, 0, 0) * (1.0 / FD**0.5)
    kernel = (1.0 + scaled + 0.5 * scaled * scaled) * reach
    tree_den = jnp.sum(kernel, axis=0, keepdims=True)
    tree_num = dot(v, kernel.astype(BF), 1, 0)
    phi = features(first[...], second[...], q, 0, NFOLD)
    high_phi = phi.astype(BF)
    low_phi = (phi - high_phi.astype(F32)).astype(BF)
    nums = []
    dens = []
    for r in range(2):
        whole = got[r].astype(F32)
        for i in range(1, got.shape[0] // 2):
            whole = whole + got[2 * i + r].astype(F32)
        high = whole.astype(BF)
        low = (whole - high.astype(F32)).astype(BF)
        both = dot(high, high_phi, 0, 0) + dot(low, high_phi, 0, 0)
        extra = dot(high, low_phi, 0, 0)
        nums.append(both[:width])
        dens.append(jnp.sum(both[width:] + extra[width:], axis=0, keepdims=True))
    lane = iota(nums[0].shape, 1)
    num = jnp.where(lane < half, nums[0], nums[1])
    den = jnp.where(lane[0:1] < half, dens[0], dens[1])
    mixed[...] = ((num + tree_num) / (den + tree_den)).astype(BF)


def page_kernel(keys, vals, path, first2, second2, first1, second1, states, norms):
    k = keys[...]
    phi = features(first2[...], second2[...], k, 1, F)
    mask = jnp.where(iota(phi.shape, 0) % 2 == 0, path[0:1], path[1:2])
    weighted = phi.astype(BF) * mask.astype(BF)
    states[...] = dot(weighted, vals[...], 1, 1).astype(BF)
    phi1 = features(first1[...], second1[...], k, 0, F)
    norms[...] = dot(path[...], phi1, 1, 1, HI)


def mlp_kernel(row_ref, w_out_far, w_gate_far, w_up_far, w_down_far, mixed, hidden, gain,
               down, residual_own, residual, attn, w_out, w_gate, w_up, w_down, sems):
    n = gain.shape[0]
    parts = sems.shape[0] - 3
    size = w_out.shape[0] // parts
    spans = [pl.ds(c * size, size) for c in range(parts)]
    copies = [
        pltpu.make_async_copy(w_out_far.at[span], w_out.at[span], sems.at[c])
        for c, span in enumerate(spans)
    ] + [
        pltpu.make_async_copy(far, near, sems.at[parts + i])
        for i, (far, near) in enumerate(
            ((w_gate_far, w_gate), (w_up_far, w_up), (w_down_far, w_down))
        )
    ]
    for copy in copies:
        copy.start()
    cols = gain_columns(gain)
    for c, span in enumerate(spans):
        copies[c].wait()
        part = dot(mixed[span], w_out[span], 0, 0)
        if c == 0:
            attn[...] = part
        else:
            attn[...] += part
    total = jnp.zeros((1, 128), F32)
    for j in range(n):
        rows = slice(j * 128, (j + 1) * 128)
        block = hidden[rows].astype(F32) + attn[:, rows].T
        residual[rows] = block
        total = total + jnp.sum(block * block, axis=0, keepdims=True)
    own = residual_own.shape[0]
    residual_own[...] = residual[pl.ds(pl.multiple_of(row_ref[0] * own, 8), own)]
    scale = lax.rsqrt(total / (n * 128) + EPS)
    normed = jnp.concatenate(
        [
            (residual[j * 128 : (j + 1) * 128] * scale * cols[:, j : j + 1]).astype(BF)
            for j in range(n)
        ],
        axis=0,
    )
    copies[parts].wait()
    gate = dot(w_gate[...], normed, 1, 0)
    copies[parts + 1].wait()
    up = dot(w_up[...], normed, 1, 0)
    active = (gate / (1.0 + jnp.exp(-gate)) * up).astype(BF)
    copies[parts + 2].wait()
    down[...] = dot(w_down[...], active, 0, 0).astype(BF)


def last_kernel(parts, residual_own, out):
    total = residual_own[...]
    for g in range(parts.shape[0]):
        total = total + parts[g].astype(F32)
    out[...] = total.astype(BF)


def call(kernel, n_smem, args, outs, scratch=(), **extra):
    return pl.pallas_call(
        kernel,
        out_shape=outs,
        in_specs=[SMEM] * n_smem + [VMEM] * (len(args) - n_smem),
        out_specs=jax.tree.map(lambda _: VMEM, outs),
        scratch_shapes=scratch,
        compiler_params=PARAMS,
        **extra,
    )(*args)


def in_vmem(x):
    return pltpu.with_memory_space_constraint(x, pltpu.VMEM)


def shape(dims, dtype):
    return jax.ShapeDtypeStruct(dims, dtype)


def local(
    hidden_in,
    attn_gain,
    mlp_gain,
    w_query,
    w_key,
    w_value,
    w_out,
    w_gate,
    w_up,
    w_down,
    page_states,
    page_norms,
    page_home,
    page_request,
    parents,
    accepted,
):
    n_row = lax.axis_size("row")
    n_col = lax.axis_size(COL)
    tok, own = hidden_in.shape
    width = n_row * own
    value_width = w_value.shape[1]
    slot_count = page_states.shape[0]
    row = lax.axis_index("row").astype(jnp.int32).reshape(1)
    first, second, fold = fold_tables()
    first1, second1 = full_tables(1, 280)
    first2, second2 = full_tables(2, 560)
    first, second, first1, second1, first2, second2 = (
        jnp.asarray(t, BF) for t in (first, second, first1, second1, first2, second2)
    )

    half = w_out.shape[0] // 2
    half_out = lax.dynamic_slice_in_dim(w_out, lax.axis_index("core") * half, half, 0)
    all_out = lax.all_gather(half_out, ("row", "core"), axis=0, tiled=True)

    packed = pl.pallas_call(
        pack_kernel,
        out_shape=shape((2 * n_col, RFOLD, 128), BF),
        in_specs=[SMEM] * 2 + [ANY] + [VMEM] * 2,
        out_specs=ANY,
        scratch_shapes=(
            pltpu.VMEM((F, slot_count, value_width), BF),
            pltpu.VMEM((RFOLD, slot_count, value_width), BF),
            pltpu.VMEM((slot_count, RFOLD, 128), BF),
            pltpu.VMEM((8, RFOLD, 128), BF),
            pltpu.SemaphoreType.DMA((1 + 2 * n_col // 8 + slot_count,)),
        ),
        compiler_params=PARAMS,
    )(
        page_home.reshape(slot_count),
        page_request,
        jnp.transpose(page_states[:, 0], (1, 0, 2)),
        page_norms,
        jnp.asarray(fold, F32),
    )
    packed, hidden_t = lax.optimization_barrier((packed, hidden_in.T))
    got = lax.all_to_all(packed, COL, split_axis=0, concat_axis=0, tiled=True)
    hidden = in_vmem(lax.all_gather(hidden_t, "row", axis=0, tiled=True))

    mixed_own, keys, vals, path = pl.pallas_call(
        mix_kernel,
        out_shape=(
            shape((value_width, tok), BF),
            shape((FD, tok), BF),
            shape((value_width, tok), BF),
            shape((8, tok), F32),
        ),
        in_specs=[SMEM] + [VMEM] * 9,
        out_specs=(VMEM,) * 4,
        compiler_params=PARAMS,
    )(
        accepted,
        in_vmem(got),
        hidden,
        attn_gain.reshape(-1, 128),
        w_query.T,
        w_key.T,
        w_value.T,
        parents,
        first,
        second,
    )

    mixed = in_vmem(lax.all_gather(mixed_own, "row", axis=0, tiled=True))

    states, norms = call(
        page_kernel,
        0,
        (keys, vals, path, first2, second2, first1, second1),
        (shape((560, value_width), BF), shape((8, 280), F32)),
    )

    down, residual_own = pl.pallas_call(
        mlp_kernel,
        out_shape=(pltpu.VMEM((width, tok), BF), pltpu.VMEM((own, tok), F32)),
        in_specs=[SMEM] + [ANY] * 4 + [VMEM] * 3,
        out_specs=(VMEM,) * 2,
        scratch_shapes=(
            pltpu.VMEM((width, tok), F32),
            pltpu.VMEM((tok, width), F32),
            pltpu.VMEM((width, width), BF),
            pltpu.VMEM(w_gate.shape[::-1], BF),
            pltpu.VMEM(w_up.shape[::-1], BF),
            pltpu.VMEM(w_down.shape, BF),
            pltpu.SemaphoreType.DMA((7,)),
        ),
        compiler_params=PARAMS,
    )(
        row,
        all_out,
        w_gate.T,
        w_up.T,
        w_down,
        mixed,
        hidden,
        mlp_gain.reshape(-1, 128),
    )
    parts = lax.all_to_all(
        down.reshape(n_row, own, tok), "row", split_axis=0, concat_axis=0, tiled=True
    )
    hidden_out = call(last_kernel, 0, (in_vmem(parts), in_vmem(residual_own)), shape((own, tok), BF)).T
    new_states = jnp.transpose(states[: 2 * F].reshape(F, 2, value_width), (1, 0, 2))[:, None]
    new_norms = norms[:2, :F][:, None]
    return (hidden_out, new_states, new_norms)


def solution(mesh):
    devices = mesh.devices
    mesh = Mesh(devices.reshape(devices.shape[0], -1, 2), ("row",) + COL)
    return jax.shard_map(
        local,
        mesh=mesh,
        in_specs=(
            P(COL, "row"),
            P(),
            P(),
            P(None, "row"),
            P(None, "row"),
            P(None, "row"),
            P("row", None),
            P(None, "row"),
            P(None, "row"),
            P("row", None),
            P(COL, "row", None, None),
            P(COL, "row", None),
            P(COL, None),
            P(COL),
            P(COL, None),
            P(COL),
        ),
        out_specs=(P(COL, "row"), P(COL, "row", None, None), P(COL, "row", None)),
        check_vma=False,
    )
```
